32 devices in a mesh: member: 8 (over z, x), space: 4 (over y, core).
Axes of the slice: x: 2, y: 2, z: 4, core: 2. Of those that a mesh axis runs over, the one named last changes fastest.
Arguments:
- states: float32 [1024, 24576], P('member', 'space'), may hold values from -6 to 6
- obs_values: float32 [2, 2048], replicated, may hold values from -6 to 6
- obs_weights: float32 [2, 2048], replicated, may hold values from 0.2 to 2
- obs_cell: int32 [2, 4, 4], P(None, 'space'), may hold values from 0 to 47
- op_select: int32 [2, 4, 4], P(None, 'space'), may hold values from 0 to 7
- op_table: float32 [8, 128, 128], replicated, may hold values from -0.5 to 0.5
- loc_obs: int32 [2, 4, 48, 8], P(None, 'space', 'member'), may hold values from 0 to 11
- loc_tile: int32 [2, 4, 48, 8], P(None, 'space', 'member'), may hold values from 0 to 7
- loc_tiles: float32 [8, 128, 128], replicated, may hold values from 0 to 1
Outputs:
- analysis: float32 [1024, 24576], P('member', 'space')
The draws below stay inside these ranges and needn't reach their ends.
All inputs are finite; a program needn't handle non-finite values.
Results may differ from the reference program's by a relative error of at most 0.00012.
Values sent between devices are 32-bit elements; how exact they have to be, the bound alone decides.
A program may use at most 128 MiB of HBM per device.

```python
import math
import jax
import jax.numpy as jnp
from jax import lax

K = 1024
BLK = 128
OB = 4
LOC = 8
NH = 8
NT = 8
BATCHES = 2
NB = 48
NCELLS = 24576
NOB = 16
N_SPACE = 4


def plant(entries, stream_key, smallest, largest):
    shape = entries.shape
    place = [jax.random.randint(jax.random.fold_in(stream_key, axis), (), 0, shape[axis]) for axis in range(len(shape))]
    entries = entries.at[tuple(place)].set(smallest)
    longest = shape.index(max(shape))
    place[longest] = (place[longest] + 1) % shape[longest]
    return entries.at[tuple(place)].set(largest)


def block_levels(stream_key, dims, shards, smallest, largest):
    def one(axis_at, blocks):
        heights = jax.random.uniform(jax.random.fold_in(jax.random.fold_in(stream_key, 6), axis_at), (blocks,), jnp.float32, smallest / len(shards), largest / len(shards))
        return jnp.repeat(jnp.exp(heights), dims[axis_at] // blocks).reshape((-1,) + (1,) * (len(dims) - axis_at - 1))

    level = one(*shards[0])
    for cut in shards[1:]:
        level = level * one(*cut)
    return level


def scatter_about(stream_key, extent, scale, bound, shards=(), dtype=jnp.bfloat16):
    factor_of = block_levels(stream_key, extent, shards, -0.22, 0.18) if shards else 1.0
    entries = jax.random.normal(stream_key, extent, jnp.float32) * scale * factor_of
    return jnp.minimum(jnp.maximum(entries, -bound), bound).astype(dtype)


def setup_inputs(seed: int = 0) -> dict:
    splits = jax.random.split(jax.random.key(seed), 10)
    return {
        "states": scatter_about(splits[0], (K, NCELLS), 1.0, 6.0, ((0, 8), (1, 4)), jnp.float32),
        "obs_values": scatter_about(splits[1], (BATCHES, NOB * BLK), 1.0, 6.0, (), jnp.float32),
        "obs_weights": jnp.clip(jnp.exp(jax.random.uniform(splits[2], (BATCHES, NOB * BLK), jnp.float32, math.log(0.2), math.log(2.0))), 0.2, 2.0),
        "obs_cell": plant(jax.random.randint(splits[3], (BATCHES, N_SPACE, OB), 0, NB), jax.random.fold_in(splits[3], 1), 0, NB - 1).astype(jnp.int32),
        "op_select": plant(jax.random.randint(splits[4], (BATCHES, N_SPACE, OB), 0, NH), jax.random.fold_in(splits[4], 1), 0, NH - 1).astype(jnp.int32),
        "op_table": scatter_about(splits[5], (NH, BLK, BLK), BLK ** -0.5, 0.5, (), jnp.float32),
        "loc_obs": plant(jax.random.randint(splits[6], (BATCHES, N_SPACE, NB, LOC), 0, 3 * OB), jax.random.fold_in(splits[6], 1), 0, (3 * OB) - 1).astype(jnp.int32),
        "loc_tile": plant(jax.random.randint(splits[7], (BATCHES, N_SPACE, NB, LOC), 0, NT), jax.random.fold_in(splits[7], 1), 0, NT - 1).astype(jnp.int32),
        "loc_tiles": jnp.clip(jax.random.uniform(splits[8], (NT, BLK, BLK), jnp.float32, 0.0, 1.0), 0.0, 1.0),
    }


def observe(blocks, obs_cell, op_select, op_table, batch_no):
    parts = []
    for slab_no in range(N_SPACE):
        picked = blocks[:, slab_no][:, obs_cell[batch_no, slab_no]]
        operators = op_table[op_select[batch_no, slab_no]]
        parts.append(jnp.einsum("koc,opc->kop", picked, operators, precision=lax.Precision.HIGHEST))
    return jnp.concatenate(parts, axis=1)


def reference(states, obs_values, obs_weights, obs_cell, op_select, op_table, loc_obs, loc_tile, loc_tiles):
    ensemble = states.reshape(K, N_SPACE, NB, BLK)
    for batch_no in range(BATCHES):
        observed = observe(ensemble, obs_cell, op_select, op_table, batch_no)
        obs_mean = jnp.mean(observed, axis=0)
        obs_anom = observed - obs_mean
        values = obs_values[batch_no].reshape(NOB, BLK)
        weights = obs_weights[batch_no].reshape(NOB, BLK)
        innov = weights * (values - obs_mean) - 0.5 * weights * obs_anom
        state_mean = jnp.mean(ensemble, axis=0)
        slabs = []
        for slab_no in range(N_SPACE):
            order = [(slab_no - 1) % N_SPACE, slab_no, (slab_no + 1) % N_SPACE]
            anom_win = jnp.concatenate([obs_anom[:, q * OB:(q + 1) * OB] for q in order], axis=1)
            innov_win = jnp.concatenate([innov[:, q * OB:(q + 1) * OB] for q in order], axis=1)

            def update_block(packed):
                cell_blk, mean_blk, reach, tile_pick = packed
                state_anom = cell_blk - mean_blk
                chosen = anom_win[:, reach]
                covariance = jnp.einsum("kc,klo->lco", state_anom, chosen, precision=lax.Precision.HIGHEST) / (K - 1)
                gain = loc_tiles[tile_pick] * covariance
                increment = jnp.einsum("klo,lco->kc", innov_win[:, reach], gain, precision=lax.Precision.HIGHEST)
                return cell_blk + increment

            fresh = lax.map(update_block, (ensemble[:, slab_no].transpose(1, 0, 2), state_mean[slab_no], loc_obs[batch_no, slab_no], loc_tile[batch_no, slab_no]))
            slabs.append(fresh.transpose(1, 0, 2))
        ensemble = jnp.stack(slabs, axis=1)
    return ensemble.reshape(K, NCELLS)
```

```python
import functools

import jax
import jax.numpy as jnp
from jax import lax
from jax.experimental import pallas as pl
from jax.experimental.pallas import tpu as pltpu
from jax.sharding import PartitionSpec as P

BLK = 128
NT_DIMS = (((1,), (1,)), ((), ()))


def split(x):
    hi = x.astype(jnp.bfloat16)
    lo = (x - hi.astype(jnp.float32)).astype(jnp.bfloat16)
    return hi, lo


def dot(a, b):
    return jnp.dot(a, b, preferred_element_type=jnp.float32)


def dot_nt(a, b):
    return lax.dot_general(a, b, NT_DIMS, preferred_element_type=jnp.float32)


def observe(block, operator):
    hi, lo = split(block)
    op_hi, op_lo = split(operator)
    part = dot_nt(hi, jnp.concatenate([op_hi, op_lo], axis=0))
    return part[:, :BLK] + part[:, BLK:] + dot_nt(lo, op_hi)


def send(src, dst, send_sem, recv_sem, member, space):
    return pltpu.make_async_remote_copy(
        src_ref=src,
        dst_ref=dst,
        send_sem=send_sem,
        recv_sem=recv_sem,
        device_id=(member, space),
        device_id_type=pl.DeviceIdType.MESH,
    )


def columns(ref, block):
    return ref.at[:, pl.ds(pl.multiple_of(block * BLK, BLK), BLK)]


def load_window(batch, place, source, window_ref, values_ref, weights_ref, scratch):
    hi_ref, lo_ref, d_ref, w_ref = scratch[:4]
    _, ob, members, _ = window_ref.shape
    for o in range(ob):
        j = place * ob + o
        at = pl.ds(pl.multiple_of((source * ob + o) * BLK, BLK), BLK)
        weight = weights_ref[batch:batch + 1, at]
        block = window_ref[place, o]
        mean = jnp.sum(block, axis=0, keepdims=True) * (1.0 / members)
        hi, lo = split(block - mean)
        hi_ref[j] = hi
        lo_ref[j] = lo
        w_ref[j] = weight
        d_ref[j] = weight * (values_ref[batch:batch + 1, at] - mean)


def update(cell, picks, tiles_ref, scratch, acc_ref):
    hi_ref, lo_ref, d_ref, w_ref = scratch
    members = cell.shape[0]
    mean = jnp.sum(cell, axis=0, keepdims=True) * (1.0 / members)
    hi, lo = split(jnp.transpose(cell - mean))
    both = jnp.concatenate([hi, lo], axis=0)
    ones = []
    for pair in range(len(picks) // 2):
        (first, tile_a), (second, tile_b) = picks[2 * pair], picks[2 * pair + 1]
        obs_hi = jnp.concatenate([hi_ref[first], hi_ref[second]], axis=1)
        obs_lo = jnp.concatenate([lo_ref[first], lo_ref[second]], axis=1)
        part = dot(both, obs_hi)
        cov = part[:BLK] + part[BLK:] + dot(hi, obs_lo)
        tile = jnp.concatenate([tiles_ref[tile_a], tiles_ref[tile_b]], axis=1)
        gain = tile * (cov * (1.0 / (members - 1)))
        d = jnp.concatenate([d_ref[first], d_ref[second]], axis=1)
        w = jnp.concatenate([w_ref[first], w_ref[second]], axis=1)
        ones.append(jnp.sum(gain * d, axis=1, keepdims=True))
        gain_hi, gain_lo = split(gain * (-0.5 * w))
        step = dot_nt(obs_hi, jnp.concatenate([gain_hi, gain_lo], axis=0))
        step = step[:, :BLK] + step[:, BLK:] + dot_nt(obs_lo, gain_hi)
        if pair == 0:
            acc_ref[...] = step
        else:
            acc_ref[...] += step
    shift = functools.reduce(jnp.add, ones)
    row = jnp.transpose(jnp.broadcast_to(shift, (BLK, BLK)))[:1]
    return cell + (acc_ref[...] + row)


def kernel(member_n, space_n, *refs):
    cell_ref, op_ref, reach_ref, tile_ref, reach_src, tile_src = refs[:6]
    states_hbm, values_ref, weights_ref, table_ref, tiles_ref, out_ref = refs[6:12]
    states_ref, cells_ref, picks_ref, win1_ref, win2_ref, acc_ref = refs[12:18]
    ints_ref, table_of_ints, scratch1, scratch2 = refs[18], refs[19], refs[20:24], refs[24:28]
    load_sem, local_sem, ints_send, ints_recv, hop_send, hop_recv, halo_send, halo_recv = refs[28:36]
    in_send, in_recv, in_local, back_send, back_recv, out_send, out_recv, out_local = refs[36:]

    nb, members, _ = cells_ref.shape
    ob, loc = picks_ref.shape[0], reach_ref.shape[3]
    share = states_ref.shape[1]
    me = lax.axis_index("member")
    slab = lax.axis_index("space")
    after = lax.rem(slab + 1, space_n)
    before = lax.rem(slab + space_n - 1, space_n)
    line = member_n // 2
    at, lane = me // 2, lax.rem(me, 2)
    mate = at * 2 + 1 - lane

    def load(block):
        return pltpu.make_async_copy(
            columns(states_hbm, block), states_ref.at[block], load_sem.at[block]
        )

    @pl.loop(0, member_n * nb)
    def _(block):
        load(block).start()

    barrier = pltpu.get_barrier_semaphore()

    def greet(member, space):
        pl.semaphore_signal(
            barrier, inc=1, device_id=(member, space), device_id_type=pl.DeviceIdType.MESH
        )

    greet(me, after)
    greet(me, before)
    for hop_by in range(1, member_n):
        greet(lax.rem(me + hop_by, member_n), slab)

    def rows(member):
        return pl.ds(pl.multiple_of(member * share, 8), share)

    @pl.loop(0, member_n * nb)
    def _(block):
        load(block).wait()

    own_ref = win1_ref.at[1]
    for o in range(ob):
        own_ref[o, rows(me)] = observe(states_ref[cell_ref[0, 0, o]], table_ref[op_ref[0, 0, o]])
    for o in range(ob):
        picks_ref[o, rows(me)] = states_ref[cell_ref[1, 0, o]]
    pl.semaphore_wait(barrier, member_n + 1)

    def hop(item, member, way, target):
        part = (own_ref, picks_ref)[item].at[:, rows(member)]
        return send(
            part, part, hop_send.at[item, member, way], hop_recv.at[item, member], target, slab
        )

    def side(member, way):
        return send(
            own_ref.at[:, rows(member)],
            win1_ref.at[2 * way, :, rows(member)],
            halo_send.at[member, way],
            halo_recv.at[member, way],
            me,
            (after, before)[way],
        )

    def pass_on(item, member, up, down, across):
        if up:
            @pl.when(at < line - 1)
            def _():
                hop(item, member, 0, me + 2).start()

        if down:
            @pl.when(at > 0)
            def _():
                hop(item, member, 1, me - 2).start()

        if across:
            hop(item, member, 2, mate).start()
        if item == 0:
            side(member, 0).start()
            side(member, 1).start()

    def landed(item, member):
        hop(item, member, 2, mate).wait_recv()

    def take(block, hop_by):
        peer = lax.rem(me + hop_by, member_n)
        return send(
            states_ref.at[peer * nb + block],
            cells_ref.at[block, rows(me)],
            in_send.at[block, hop_by],
            in_recv.at[block, me],
            peer,
            slab,
        )

    def stay(block):
        return pltpu.make_async_copy(
            states_ref.at[me * nb + block], cells_ref.at[block, rows(me)], in_local.at[block]
        )

    hops = sorted(range(1, member_n), key=lambda k: (abs(k - line), k))

    def swap_in(block):
        for hop_by in hops:
            take(block, hop_by).start()
        stay(block).start()

    def give_ints(which, hop_by):
        peer = lax.rem(me + hop_by, member_n)
        return send(
            (reach_src, tile_src)[which].at[0, 0],
            ints_ref.at[which, me],
            ints_send.at[which, hop_by],
            ints_recv.at[which, me],
            peer,
            slab,
        )

    def keep_ints(which):
        return pltpu.make_async_copy(
            (reach_src, tile_src)[which].at[0, 0], ints_ref.at[which, me], local_sem.at[1 + which]
        )

    pass_on(0, me, True, True, True)
    for which in range(2):
        for hop_by in range(1, member_n):
            give_ints(which, hop_by).start()
        keep_ints(which).start()
    pass_on(1, me, True, True, True)
    swap_in(0)

    for item in range(2):
        for step in range(1, line):
            low, high = me - 2 * step, me + 2 * step

            @pl.when(low >= 0)
            def _():
                landed(item, low)
                pass_on(item, low, True, False, True)

            @pl.when(high < member_n)
            def _():
                landed(item, high)
                pass_on(item, high, False, True, True)

            far = 2 * (step - 1)
            if far == 0:
                landed(item, mate)
                pass_on(item, mate, False, False, False)
            else:
                @pl.when(mate - far >= 0)
                def _():
                    landed(item, mate - far)
                    pass_on(item, mate - far, False, False, False)

                @pl.when(mate + far < member_n)
                def _():
                    landed(item, mate + far)
                    pass_on(item, mate + far, False, False, False)

        far = 2 * (line - 1)

        @pl.when(mate - far >= 0)
        def _():
            landed(item, mate - far)
            pass_on(item, mate - far, False, False, False)

        @pl.when(mate + far < member_n)
        def _():
            landed(item, mate + far)
            pass_on(item, mate + far, False, False, False)

        if item == 0:
            swap_in(1)

    @pl.loop(2, nb)
    def _(block):
        swap_in(block)

    for which in range(2):
        keep_ints(which).wait()
        for hop_by in range(1, member_n):
            peer = lax.rem(me + hop_by, member_n)
            send(
                (reach_src, tile_src)[which].at[0, 0],
                ints_ref.at[which, peer],
                ints_send.at[which, hop_by],
                ints_recv.at[which, peer],
                peer,
                slab,
            ).wait_recv()
    scalars = pltpu.make_async_copy(ints_ref, table_of_ints, local_sem.at[3])
    scalars.start()

    near = 2 * (1 - lax.rem(slab, 2))
    far = 2 - near

    def source_of(place):
        return lax.rem(slab + space_n - 1 + place, space_n)

    load_window(0, 1, slab, win1_ref, values_ref, weights_ref, scratch1)
    for way in range(2):
        for member in range(member_n):
            side(member, way).wait_recv()
    for place in (near, far):
        load_window(0, place, source_of(place), win1_ref, values_ref, weights_ref, scratch1)
    scalars.wait()

    def back(o, way):
        return send(
            win2_ref.at[1, o],
            win2_ref.at[2 * way, o],
            back_send.at[o, way],
            back_recv.at[o, way],
            me,
            (after, before)[way],
        )

    @pl.loop(0, ob)
    def _(o):
        cell = cell_ref[1, 0, o]
        owner = cell // nb
        place = cell - owner * nb
        picks = [
            (table_of_ints[0, owner, place, l], table_of_ints[1, owner, place, l])
            for l in range(loc)
        ]
        fresh = update(picks_ref[o], picks, tiles_ref, scratch1, acc_ref)
        win2_ref[1, o] = observe(fresh, table_ref[op_ref[1, 0, o]])
        back(o, 0).start()
        back(o, 1).start()

    @pl.loop(0, nb)
    def _(block):
        stay(block).wait()
        for hop_by in range(1, member_n):
            peer = lax.rem(me + hop_by, member_n)
            send(
                states_ref.at[peer * nb + block],
                cells_ref.at[block, rows(peer)],
                in_send.at[block, hop_by],
                in_recv.at[block, peer],
                peer,
                slab,
            ).wait_recv()
        picks = [(reach_ref[0, 0, block, l], tile_ref[0, 0, block, l]) for l in range(loc)]
        cells_ref[block] = update(cells_ref[block], picks, tiles_ref, scratch1, acc_ref)

    load_window(1, 1, slab, win2_ref, values_ref, weights_ref, scratch2)
    for way in range(2):
        for o in range(ob):
            back(o, way).wait_recv()
    for place in (near, far):
        load_window(1, place, source_of(place), win2_ref, values_ref, weights_ref, scratch2)

    def give(block, hop_by):
        peer = lax.rem(me + hop_by, member_n)
        return send(
            cells_ref.at[block, rows(peer)],
            columns(out_ref, me * nb + block),
            out_send.at[block, hop_by],
            out_recv.at[block, me],
            peer,
            slab,
        )

    def keep(block):
        return pltpu.make_async_copy(
            cells_ref.at[block, rows(me)], columns(out_ref, me * nb + block), out_local.at[block]
        )

    @pl.loop(0, nb)
    def _(block):
        picks = [(reach_ref[1, 0, block, l], tile_ref[1, 0, block, l]) for l in range(loc)]
        cells_ref[block] = update(cells_ref[block], picks, tiles_ref, scratch2, acc_ref)
        for hop_by in hops:
            give(block, hop_by).start()
        keep(block).start()

    for which in range(2):
        for hop_by in range(1, member_n):
            give_ints(which, hop_by).wait_send()
    for member in range(member_n):
        spot, same = member // 2, lane == member % 2
        for way in range(2):
            side(member, way).wait_send()
        for item in range(2):
            @pl.when(same & (spot <= at) & (at < line - 1))
            def _():
                hop(item, member, 0, mate).wait_send()

            @pl.when(same & (spot >= at) & (at > 0))
            def _():
                hop(item, member, 1, mate).wait_send()

            @pl.when(same)
            def _():
                hop(item, member, 2, mate).wait_send()
    for o in range(ob):
        for way in range(2):
            back(o, way).wait_send()

    @pl.loop(0, nb)
    def _(block):
        keep(block).wait()
        for hop_by in range(1, member_n):
            take(block, hop_by).wait_send()
            give(block, hop_by).wait_send()
            peer = lax.rem(me + hop_by, member_n)
            send(
                cells_ref.at[block, rows(peer)],
                columns(out_ref, peer * nb + block),
                out_send.at[block, hop_by],
                out_recv.at[block, peer],
                peer,
                slab,
            ).wait_recv()


def per_device(
    states, obs_values, obs_weights, obs_cell, op_select, op_table, loc_obs, loc_tile, loc_tiles
):
    member_n, space_n = lax.axis_size("member"), lax.axis_size("space")
    share, width = states.shape
    members = share * member_n
    ob = obs_cell.shape[2]
    nb, loc = loc_obs.shape[2:]
    f32, bf16, i32 = jnp.float32, jnp.bfloat16, jnp.int32
    smem = pl.BlockSpec(memory_space=pltpu.SMEM)
    vmem = pl.BlockSpec(memory_space=pltpu.VMEM)
    anywhere = pl.BlockSpec(memory_space=pl.ANY)
    dma = pltpu.SemaphoreType.DMA
    parts = [
        pltpu.VMEM((3 * ob, members, BLK), bf16),
        pltpu.VMEM((3 * ob, members, BLK), bf16),
        pltpu.VMEM((3 * ob, 1, BLK), f32),
        pltpu.VMEM((3 * ob, 1, BLK), f32),
    ]
    return pl.pallas_call(
        functools.partial(kernel, member_n, space_n),
        out_shape=jax.ShapeDtypeStruct((share, width), f32),
        in_specs=[smem] * 4 + [vmem] * 2 + [anywhere] + [vmem] * 4,
        out_specs=anywhere,
        scratch_shapes=[
            pltpu.VMEM((width // BLK, share, BLK), f32),
            pltpu.VMEM((nb, members, BLK), f32),
            pltpu.VMEM((ob, members, BLK), f32),
            pltpu.VMEM((3, ob, members, BLK), f32),
            pltpu.VMEM((3, ob, members, BLK), f32),
            pltpu.VMEM((members, BLK), f32),
            pltpu.VMEM((2, member_n, nb, loc), i32),
            pltpu.SMEM((2, member_n, nb, loc), i32),
        ] + parts + parts + [
            dma((width // BLK,)),
            dma((4,)),
            dma((2, member_n)),
            dma((2, member_n)),
            dma((2, member_n, 3)),
            dma((2, member_n)),
            dma((member_n, 2)),
            dma((member_n, 2)),
            dma((nb, member_n)),
            dma((nb, member_n)),
            dma((nb,)),
            dma((ob, 2)),
            dma((ob, 2)),
            dma((nb, member_n)),
            dma((nb, member_n)),
            dma((nb,)),
        ],
        compiler_params=pltpu.CompilerParams(
            vmem_limit_bytes=58 * 1024 * 1024, collective_id=0, has_side_effects=True
        ),
    )(
        obs_cell, op_select, loc_obs, loc_tile, loc_obs, loc_tile,
        states, obs_values, obs_weights, op_table, loc_tiles,
    )


def solution(mesh):
    placed = (
        P("member", "space"),
        P(),
        P(),
        P(None, "space", None),
        P(None, "space", None),
        P(),
        P(None, "space", "member", None),
        P(None, "space", "member", None),
        P(),
    )
    return jax.shard_map(
        per_device, mesh=mesh, in_specs=placed, out_specs=P("member", "space"), check_vma=False
    )
```

```python
import functools

import jax
import jax.numpy as jnp
from jax import lax
from jax.experimental import pallas as pl
from jax.experimental.pallas import tpu as pltpu
from jax.sharding import PartitionSpec as P

BLK = 128
NT_DIMS = (((1,), (1,)), ((), ()))


def split(x):
    hi = x.astype(jnp.bfloat16)
    lo = (x - hi.astype(jnp.float32)).astype(jnp.bfloat16)
    return hi, lo


def dot(a, b):
    return jnp.dot(a, b, preferred_element_type=jnp.float32)


def dot_nt(a, b):
    return lax.dot_general(a, b, NT_DIMS, preferred_element_type=jnp.float32)


def observe(block, operator):
    hi, lo = split(block)
    op_hi, op_lo = split(operator)
    part = dot_nt(hi, jnp.concatenate([op_hi, op_lo], axis=0))
    return part[:, :BLK] + part[:, BLK:] + dot_nt(lo, op_hi)


def send(src, dst, send_sem, recv_sem, member, space):
    return pltpu.make_async_remote_copy(
        src_ref=src,
        dst_ref=dst,
        send_sem=send_sem,
        recv_sem=recv_sem,
        device_id=(member, space),
        device_id_type=pl.DeviceIdType.MESH,
    )


def columns(ref, block):
    return ref.at[:, pl.ds(pl.multiple_of(block * BLK, BLK), BLK)]


def load_window(batch, place, source, window_ref, values_ref, weights_ref, scratch):
    hi_ref, lo_ref, d_ref, w_ref = scratch[:4]
    _, ob, members, _ = window_ref.shape
    for o in range(ob):
        j = place * ob + o
        at = pl.ds(pl.multiple_of((source * ob + o) * BLK, BLK), BLK)
        weight = weights_ref[batch:batch + 1, at]
        block = window_ref[place, o]
        mean = jnp.sum(block, axis=0, keepdims=True) * (1.0 / members)
        hi, lo = split(block - mean)
        hi_ref[j] = hi
        lo_ref[j] = lo
        w_ref[j] = weight
        d_ref[j] = weight * (values_ref[batch:batch + 1, at] - mean)


def update(cell, picks, tiles_ref, scratch, acc_ref):
    hi_ref, lo_ref, d_ref, w_ref = scratch
    members = cell.shape[0]
    mean = jnp.sum(cell, axis=0, keepdims=True) * (1.0 / members)
    hi, lo = split(jnp.transpose(cell - mean))
    both = jnp.concatenate([hi, lo], axis=0)
    ones = []
    for pair in range(len(picks) // 2):
        (first, tile_a), (second, tile_b) = picks[2 * pair], picks[2 * pair + 1]
        obs_hi = jnp.concatenate([hi_ref[first], hi_ref[second]], axis=1)
        obs_lo = jnp.concatenate([lo_ref[first], lo_ref[second]], axis=1)
        part = dot(both, obs_hi)
        cov = part[:BLK] + part[BLK:] + dot(hi, obs_lo)
        tile = jnp.concatenate([tiles_ref[tile_a], tiles_ref[tile_b]], axis=1)
        gain = tile * (cov * (1.0 / (members - 1)))
        d = jnp.concatenate([d_ref[first], d_ref[second]], axis=1)
        w = jnp.concatenate([w_ref[first], w_ref[second]], axis=1)
        ones.append(jnp.sum(gain * d, axis=1, keepdims=True))
        gain_hi, gain_lo = split(gain * (-0.5 * w))
        step = dot_nt(obs_hi, jnp.concatenate([gain_hi, gain_lo], axis=0))
        step = step[:, :BLK] + step[:, BLK:] + dot_nt(obs_lo, gain_hi)
        if pair == 0:
            acc_ref[...] = step
        else:
            acc_ref[...] += step
    shift = functools.reduce(jnp.add, ones)
    row = jnp.transpose(jnp.broadcast_to(shift, (BLK, BLK)))[:1]
    return cell + (acc_ref[...] + row)


def kernel(member_n, space_n, *refs):
    cell_ref, op_ref, reach_ref, tile_ref, reach_src, tile_src = refs[:6]
    states_hbm, values_ref, weights_ref, table_ref, tiles_ref, out_ref = refs[6:12]
    states_ref, cells_ref, picks_ref, win1_ref, win2_ref, acc_ref = refs[12:18]
    ints_ref, table_of_ints, scratch1, scratch2 = refs[18], refs[19], refs[20:24], refs[24:28]
    load_sem, local_sem, ints_send, ints_recv, hop_send, hop_recv, halo_send, halo_recv = refs[28:36]
    in_send, in_recv, in_local, back_send, back_recv, out_send, out_recv, out_local = refs[36:]

    nb, members, _ = cells_ref.shape
    ob, loc = picks_ref.shape[0], reach_ref.shape[3]
    share = states_ref.shape[1]
    me = lax.axis_index("member")
    slab = lax.axis_index("space")
    after = lax.rem(slab + 1, space_n)
    before = lax.rem(slab + space_n - 1, space_n)
    line = member_n // 2
    at, lane = me // 2, lax.rem(me, 2)
    mate = at * 2 + 1 - lane

    def load(block):
        return pltpu.make_async_copy(
            columns(states_hbm, block), states_ref.at[block], load_sem.at[block]
        )

    @pl.loop(0, member_n * nb)
    def _(block):
        load(block).start()

    barrier = pltpu.get_barrier_semaphore()

    def greet(member, space):
        pl.semaphore_signal(
            barrier, inc=1, device_id=(member, space), device_id_type=pl.DeviceIdType.MESH
        )

    greet(me, after)
    greet(me, before)
    for hop_by in range(1, member_n):
        greet(lax.rem(me + hop_by, member_n), slab)

    def rows(member):
        return pl.ds(pl.multiple_of(member * share, 8), share)

    @pl.loop(0, member_n * nb)
    def _(block):
        load(block).wait()

    own_ref = win1_ref.at[1]
    for o in range(ob):
        own_ref[o, rows(me)] = observe(states_ref[cell_ref[0, 0, o]], table_ref[op_ref[0, 0, o]])
    for o in range(ob):
        picks_ref[o, rows(me)] = states_ref[cell_ref[1, 0, o]]
    pl.semaphore_wait(barrier, member_n + 1)

    def hop(item, member, way, target):
        part = (own_ref, picks_ref)[item].at[:, rows(member)]
        return send(
            part, part, hop_send.at[item, member, way], hop_recv.at[item, member], target, slab
        )

    def side(member, way):
        return send(
            own_ref.at[:, rows(member)],
            win1_ref.at[2 * way, :, rows(member)],
            halo_send.at[member, way],
            halo_recv.at[member, way],
            me,
            (after, before)[way],
        )

    def pass_on(item, member, up, down, across):
        if up:
            @pl.when(at < line - 1)
            def _():
                hop(item, member, 0, me + 2).start()

        if down:
            @pl.when(at > 0)
            def _():
                hop(item, member, 1, me - 2).start()

        if across:
            hop(item, member, 2, mate).start()
        if item == 0:
            side(member, 0).start()
            side(member, 1).start()

    def landed(item, member):
        hop(item, member, 2, mate).wait_recv()

    def take(block, hop_by):
        peer = lax.rem(me + hop_by, member_n)
        return send(
            states_ref.at[peer * nb + block],
            cells_ref.at[block, rows(me)],
            in_send.at[block, hop_by],
            in_recv.at[block, me],
            peer,
            slab,
        )

    def stay(block):
        return pltpu.make_async_copy(
            states_ref.at[me * nb + block], cells_ref.at[block, rows(me)], in_local.at[block]
        )

    hops = sorted(range(1, member_n), key=lambda k: (abs(k - line), k))

    def straight(block):
        for hop_by in hops:
            if hop_by % 2 == 0:
                take(block, hop_by).start()
        stay(block).start()

    def crossing(block):
        for hop_by in hops:
            if hop_by % 2 == 1:
                take(block, hop_by).start()

    def give_ints(which, hop_by):
        peer = lax.rem(me + hop_by, member_n)
        return send(
            (reach_src, tile_src)[which].at[0, 0],
            ints_ref.at[which, me],
            ints_send.at[which, hop_by],
            ints_recv.at[which, me],
            peer,
            slab,
        )

    def keep_ints(which):
        return pltpu.make_async_copy(
            (reach_src, tile_src)[which].at[0, 0], ints_ref.at[which, me], local_sem.at[1 + which]
        )

    pass_on(0, me, True, True, True)
    for which in range(2):
        for hop_by in range(1, member_n):
            give_ints(which, hop_by).start()
        keep_ints(which).start()
    pass_on(1, me, True, True, True)
    straight(0)

    for item in range(2):
        for step in range(1, line):
            low, high = me - 2 * step, me + 2 * step

            @pl.when(low >= 0)
            def _():
                landed(item, low)
                pass_on(item, low, True, False, True)

            @pl.when(high < member_n)
            def _():
                landed(item, high)
                pass_on(item, high, False, True, True)

            if step == 1:
                for b in ([1],[3])[item]:
                    straight(b)
            far = 2 * (step - 1)
            if far == 0:
                landed(item, mate)
                pass_on(item, mate, False, False, False)
            else:
                @pl.when(mate - far >= 0)
                def _():
                    landed(item, mate - far)
                    pass_on(item, mate - far, False, False, False)

                @pl.when(mate + far < member_n)
                def _():
                    landed(item, mate + far)
                    pass_on(item, mate + far, False, False, False)

        far = 2 * (line - 1)

        @pl.when(mate - far >= 0)
        def _():
            landed(item, mate - far)
            pass_on(item, mate - far, False, False, False)

        @pl.when(mate + far < member_n)
        def _():
            landed(item, mate + far)
            pass_on(item, mate + far, False, False, False)

        if item == 0:
            pass
            straight(2)

    for block in range(4, nb):
        straight(block)
    for block in range(nb):
        crossing(block)

    for which in range(2):
        keep_ints(which).wait()
        for hop_by in range(1, member_n):
            peer = lax.rem(me + hop_by, member_n)
            send(
                (reach_src, tile_src)[which].at[0, 0],
                ints_ref.at[which, peer],
                ints_send.at[which, hop_by],
                ints_recv.at[which, peer],
                peer,
                slab,
            ).wait_recv()
    scalars = pltpu.make_async_copy(ints_ref, table_of_ints, local_sem.at[3])
    scalars.start()

    near = 2 * (1 - lax.rem(slab, 2))
    far = 2 - near

    def source_of(place):
        return lax.rem(slab + space_n - 1 + place, space_n)

    load_window(0, 1, slab, win1_ref, values_ref, weights_ref, scratch1)
    for way in range(2):
        for member in range(member_n):
            side(member, way).wait_recv()
    for place in (near, far):
        load_window(0, place, source_of(place), win1_ref, values_ref, weights_ref, scratch1)
    scalars.wait()

    def back(o, way):
        return send(
            win2_ref.at[1, o],
            win2_ref.at[2 * way, o],
            back_send.at[o, way],
            back_recv.at[o, way],
            me,
            (after, before)[way],
        )

    @pl.loop(0, ob)
    def _(o):
        cell = cell_ref[1, 0, o]
        owner = cell // nb
        place = cell - owner * nb
        picks = [
            (table_of_ints[0, owner, place, l], table_of_ints[1, owner, place, l])
            for l in range(loc)
        ]
        fresh = update(picks_ref[o], picks, tiles_ref, scratch1, acc_ref)
        win2_ref[1, o] = observe(fresh, table_ref[op_ref[1, 0, o]])
        back(o, 0).start()
        back(o, 1).start()

    @pl.loop(0, nb)
    def _(block):
        stay(block).wait()
        for hop_by in range(1, member_n):
            peer = lax.rem(me + hop_by, member_n)
            send(
                states_ref.at[peer * nb + block],
                cells_ref.at[block, rows(peer)],
                in_send.at[block, hop_by],
                in_recv.at[block, peer],
                peer,
                slab,
            ).wait_recv()
        picks = [(reach_ref[0, 0, block, l], tile_ref[0, 0, block, l]) for l in range(loc)]
        cells_ref[block] = update(cells_ref[block], picks, tiles_ref, scratch1, acc_ref)

    load_window(1, 1, slab, win2_ref, values_ref, weights_ref, scratch2)
    for way in range(2):
        for o in range(ob):
            back(o, way).wait_recv()
    for place in (near, far):
        load_window(1, place, source_of(place), win2_ref, values_ref, weights_ref, scratch2)

    def give(block, hop_by):
        peer = lax.rem(me + hop_by, member_n)
        return send(
            cells_ref.at[block, rows(peer)],
            columns(out_ref, me * nb + block),
            out_send.at[block, hop_by],
            out_recv.at[block, me],
            peer,
            slab,
        )

    def keep(block):
        return pltpu.make_async_copy(
            cells_ref.at[block, rows(me)], columns(out_ref, me * nb + block), out_local.at[block]
        )

    @pl.loop(0, nb)
    def _(block):
        picks = [(reach_ref[1, 0, block, l], tile_ref[1, 0, block, l]) for l in range(loc)]
        cells_ref[block] = update(cells_ref[block], picks, tiles_ref, scratch2, acc_ref)
        for hop_by in hops:
            give(block, hop_by).start()
        keep(block).start()

    for which in range(2):
        for hop_by in range(1, member_n):
            give_ints(which, hop_by).wait_send()
    for member in range(member_n):
        spot, same = member // 2, lane == member % 2
        for way in range(2):
            side(member, way).wait_send()
        for item in range(2):
            @pl.when(same & (spot <= at) & (at < line - 1))
            def _():
                hop(item, member, 0, mate).wait_send()

            @pl.when(same & (spot >= at) & (at > 0))
            def _():
                hop(item, member, 1, mate).wait_send()

            @pl.when(same)
            def _():
                hop(item, member, 2, mate).wait_send()
    for o in range(ob):
        for way in range(2):
            back(o, way).wait_send()

    @pl.loop(0, nb)
    def _(block):
        keep(block).wait()
        for hop_by in range(1, member_n):
            take(block, hop_by).wait_send()
            give(block, hop_by).wait_send()
            peer = lax.rem(me + hop_by, member_n)
            send(
                cells_ref.at[block, rows(peer)],
                columns(out_ref, peer * nb + block),
                out_send.at[block, hop_by],
                out_recv.at[block, peer],
                peer,
                slab,
            ).wait_recv()


def per_device(
    states, obs_values, obs_weights, obs_cell, op_select, op_table, loc_obs, loc_tile, loc_tiles
):
    member_n, space_n = lax.axis_size("member"), lax.axis_size("space")
    share, width = states.shape
    members = share * member_n
    ob = obs_cell.shape[2]
    nb, loc = loc_obs.shape[2:]
    f32, bf16, i32 = jnp.float32, jnp.bfloat16, jnp.int32
    smem = pl.BlockSpec(memory_space=pltpu.SMEM)
    vmem = pl.BlockSpec(memory_space=pltpu.VMEM)
    anywhere = pl.BlockSpec(memory_space=pl.ANY)
    dma = pltpu.SemaphoreType.DMA
    parts = [
        pltpu.VMEM((3 * ob, members, BLK), bf16),
        pltpu.VMEM((3 * ob, members, BLK), bf16),
        pltpu.VMEM((3 * ob, 1, BLK), f32),
        pltpu.VMEM((3 * ob, 1, BLK), f32),
    ]
    return pl.pallas_call(
        functools.partial(kernel, member_n, space_n),
        out_shape=jax.ShapeDtypeStruct((share, width), f32),
        in_specs=[smem] * 4 + [vmem] * 2 + [anywhere] + [vmem] * 4,
        out_specs=anywhere,
        scratch_shapes=[
            pltpu.VMEM((width // BLK, share, BLK), f32),
            pltpu.VMEM((nb, members, BLK), f32),
            pltpu.VMEM((ob, members, BLK), f32),
            pltpu.VMEM((3, ob, members, BLK), f32),
            pltpu.VMEM((3, ob, members, BLK), f32),
            pltpu.VMEM((members, BLK), f32),
            pltpu.VMEM((2, member_n, nb, loc), i32),
            pltpu.SMEM((2, member_n, nb, loc), i32),
        ] + parts + parts + [
            dma((width // BLK,)),
            dma((4,)),
            dma((2, member_n)),
            dma((2, member_n)),
            dma((2, member_n, 3)),
            dma((2, member_n)),
            dma((member_n, 2)),
            dma((member_n, 2)),
            dma((nb, member_n)),
            dma((nb, member_n)),
            dma((nb,)),
            dma((ob, 2)),
            dma((ob, 2)),
            dma((nb, member_n)),
            dma((nb, member_n)),
            dma((nb,)),
        ],
        compiler_params=pltpu.CompilerParams(
            vmem_limit_bytes=58 * 1024 * 1024, collective_id=0, has_side_effects=True
        ),
    )(
        obs_cell, op_select, loc_obs, loc_tile, loc_obs, loc_tile,
        states, obs_values, obs_weights, op_table, loc_tiles,
    )


def solution(mesh):
    placed = (
        P("member", "space"),
        P(),
        P(),
        P(None, "space", None),
        P(None, "space", None),
        P(),
        P(None, "space", "member", None),
        P(None, "space", "member", None),
        P(),
    )
    return jax.shard_map(
        per_device, mesh=mesh, in_specs=placed, out_specs=P("member", "space"), check_vma=False
    )
```

```python
import functools

import jax
import jax.numpy as jnp
from jax import lax
from jax.experimental import pallas as pl
from jax.experimental.pallas import tpu as pltpu
from jax.sharding import PartitionSpec as P

BLK = 128
NT_DIMS = (((1,), (1,)), ((), ()))


def split(x):
    hi = x.astype(jnp.bfloat16)
    lo = (x - hi.astype(jnp.float32)).astype(jnp.bfloat16)
    return hi, lo


def dot(a, b):
    return jnp.dot(a, b, preferred_element_type=jnp.float32)


def dot_nt(a, b):
    return lax.dot_general(a, b, NT_DIMS, preferred_element_type=jnp.float32)


def observe(block, operator):
    hi, lo = split(block)
    op_hi, op_lo = split(operator)
    part = dot_nt(hi, jnp.concatenate([op_hi, op_lo], axis=0))
    return part[:, :BLK] + part[:, BLK:] + dot_nt(lo, op_hi)


def send(src, dst, send_sem, recv_sem, member, space):
    return pltpu.make_async_remote_copy(
        src_ref=src,
        dst_ref=dst,
        send_sem=send_sem,
        recv_sem=recv_sem,
        device_id=(member, space),
        device_id_type=pl.DeviceIdType.MESH,
    )


def columns(ref, block):
    return ref.at[:, pl.ds(pl.multiple_of(block * BLK, BLK), BLK)]


def load_window(batch, place, source, window_ref, values_ref, weights_ref, scratch):
    hi_ref, lo_ref, d_ref, w_ref = scratch[:4]
    _, ob, members, _ = window_ref.shape
    for o in range(ob):
        j = place * ob + o
        at = pl.ds(pl.multiple_of((source * ob + o) * BLK, BLK), BLK)
        weight = weights_ref[batch:batch + 1, at]
        block = window_ref[place, o]
        mean = jnp.sum(block, axis=0, keepdims=True) * (1.0 / members)
        hi, lo = split(block - mean)
        hi_ref[j] = hi
        lo_ref[j] = lo
        w_ref[j] = weight
        d_ref[j] = weight * (values_ref[batch:batch + 1, at] - mean)


def update(cell, picks, tiles_ref, scratch, acc_ref):
    hi_ref, lo_ref, d_ref, w_ref = scratch
    members = cell.shape[0]
    mean = jnp.sum(cell, axis=0, keepdims=True) * (1.0 / members)
    hi, lo = split(jnp.transpose(cell - mean))
    both = jnp.concatenate([hi, lo], axis=0)
    ones = []
    for pair in range(len(picks) // 2):
        (first, tile_a), (second, tile_b) = picks[2 * pair], picks[2 * pair + 1]
        obs_hi = jnp.concatenate([hi_ref[first], hi_ref[second]], axis=1)
        obs_lo = jnp.concatenate([lo_ref[first], lo_ref[second]], axis=1)
        part = dot(both, obs_hi)
        cov = part[:BLK] + part[BLK:] + dot(hi, obs_lo)
        tile = jnp.concatenate([tiles_ref[tile_a], tiles_ref[tile_b]], axis=1)
        gain = tile * (cov * (1.0 / (members - 1)))
        d = jnp.concatenate([d_ref[first], d_ref[second]], axis=1)
        w = jnp.concatenate([w_ref[first], w_ref[second]], axis=1)
        ones.append(jnp.sum(gain * d, axis=1, keepdims=True))
        gain_hi, gain_lo = split(gain * (-0.5 * w))
        step = dot_nt(obs_hi, jnp.concatenate([gain_hi, gain_lo], axis=0))
        step = step[:, :BLK] + step[:, BLK:] + dot_nt(obs_lo, gain_hi)
        if pair == 0:
            acc_ref[...] = step
        else:
            acc_ref[...] += step
    shift = functools.reduce(jnp.add, ones)
    row = jnp.transpose(jnp.broadcast_to(shift, (BLK, BLK)))[:1]
    return cell + (acc_ref[...] + row)


def kernel(member_n, space_n, ahead, *refs):
    sources, states_hbm, tiles_hbm, out_ref, refs = refs[:6], refs[6], refs[7], refs[8], refs[9:]
    copies, (tiles_ref, table_of_ints, ints_ref), refs = refs[:5], refs[5:8], refs[8:]
    cell_ref, op_ref, values_ref, weights_ref, table_ref = copies
    states_ref, cells_ref, picks_ref, win1_ref, win2_ref, acc_ref = refs[:6]
    scratch1, scratch2, refs = refs[6:10], refs[10:14], refs[14:]
    load_sem, local_sem, ints_send, ints_recv, hop_send, hop_recv, halo_send, halo_recv = refs[:8]
    in_send, in_recv, in_local, back_send, back_recv, rest_send, rest_recv = refs[8:15]
    out_send, out_recv, out_local = refs[15:]
    codes_hbm = sources[5]

    nb, members, _ = cells_ref.shape
    ob = picks_ref.shape[0]
    share = states_ref.shape[1]
    batches = cell_ref.shape[0]
    loc = codes_hbm.shape[1] // nb
    me = lax.axis_index("member")
    slab = lax.axis_index("space")
    after = lax.rem(slab + 1, space_n)
    before = lax.rem(slab + space_n - 1, space_n)
    line = member_n // 2
    at, lane = me // 2, lax.rem(me, 2)
    mate = at * 2 + 1 - lane
    odd = lax.rem(slab, 2)
    near, far = 2 * (1 - odd), 2 * odd
    near_slab = slab + 1 - 2 * odd
    far_slab = lax.rem(slab + space_n - 1 + 2 * odd, space_n)
    quarter = members // 4

    barrier = pltpu.get_barrier_semaphore()

    def greet(member, space):
        pl.semaphore_signal(
            barrier, inc=1, device_id=(member, space), device_id_type=pl.DeviceIdType.MESH
        )

    greet(me, after)
    greet(me, before)
    for hop_by in range(1, member_n):
        greet(lax.rem(me + hop_by, member_n), slab)

    small = [
        pltpu.make_async_copy(sources[i], copies[i], local_sem.at[i]) for i in range(len(copies))
    ]
    for copy in small:
        copy.start()

    def load(block):
        return pltpu.make_async_copy(
            columns(states_hbm, block), states_ref.at[block], load_sem.at[block]
        )

    @pl.loop(0, member_n * nb)
    def _(block):
        load(block).start()

    tiles_copy = pltpu.make_async_copy(tiles_hbm, tiles_ref, local_sem.at[5])
    tiles_copy.start()
    keep_ints = pltpu.make_async_copy(codes_hbm, ints_ref.at[me], local_sem.at[6])
    keep_ints.start()

    def rows(member):
        return pl.ds(pl.multiple_of(member * share, 8), share)

    for copy in small:
        copy.wait()

    @pl.loop(0, member_n * nb)
    def _(block):
        load(block).wait()

    own_ref = win1_ref.at[1]
    for o in range(ob):
        own_ref[o, rows(me)] = observe(states_ref[cell_ref[0, 0, o]], table_ref[op_ref[0, 0, o]])
    for o in range(ob):
        picks_ref[o, rows(me)] = states_ref[cell_ref[1, 0, o]]
    pl.semaphore_wait(barrier, member_n + 1)

    def hop(item, member, way, target):
        part = (own_ref, picks_ref)[item].at[:, rows(member)]
        return send(
            part, part, hop_send.at[item, member, way], hop_recv.at[item, member], target, slab
        )

    def side(member, way):
        return send(
            own_ref.at[:, rows(member)],
            win1_ref.at[2 * way, :, rows(member)],
            halo_send.at[member, way],
            halo_recv.at[member, way],
            me,
            (after, before)[way],
        )

    def pass_on(item, member, up, down, across):
        if up:
            @pl.when(at < line - 1)
            def _():
                hop(item, member, 0, me + 2).start()

        if down:
            @pl.when(at > 0)
            def _():
                hop(item, member, 1, me - 2).start()

        if across:
            hop(item, member, 2, mate).start()
        if item == 0:
            side(member, 0).start()
            side(member, 1).start()

    def landed(item, member):
        hop(item, member, 2, mate).wait_recv()

    def take(block, hop_by):
        peer = lax.rem(me + hop_by, member_n)
        return send(
            states_ref.at[peer * nb + block],
            cells_ref.at[block, rows(me)],
            in_send.at[block, hop_by],
            in_recv.at[block, me],
            peer,
            slab,
        )

    def stay(block):
        return pltpu.make_async_copy(
            states_ref.at[me * nb + block], cells_ref.at[block, rows(me)], in_local.at[block]
        )

    hops = sorted(range(1, member_n), key=lambda k: (abs(k - line), k))

    def straight(block):
        for hop_by in hops:
            if hop_by % 2 == 0:
                take(block, hop_by).start()
        stay(block).start()

    def crossing(block):
        for hop_by in hops:
            if hop_by % 2 == 1:
                take(block, hop_by).start()

    waiting = list(range(nb))

    def feed(count=1):
        for _ in range(min(count, len(waiting))):
            straight(waiting.pop(0))

    def give_ints(hop_by):
        peer = lax.rem(me + hop_by, member_n)
        return send(
            codes_hbm, ints_ref.at[me], ints_send.at[hop_by], ints_recv.at[me], peer, slab
        )

    pass_on(0, me, True, True, True)
    for hop_by in range(1, member_n):
        give_ints(hop_by).start()
    pass_on(1, me, True, True, True)
    feed()

    for item in range(2):
        for step in range(1, line):
            low, high = me - 2 * step, me + 2 * step

            @pl.when(low >= 0)
            def _():
                landed(item, low)
                pass_on(item, low, True, False, True)

            @pl.when(high < member_n)
            def _():
                landed(item, high)
                pass_on(item, high, False, True, True)

            if step == 1:
                feed()
            gap = 2 * (step - 1)
            if gap == 0:
                landed(item, mate)
                pass_on(item, mate, False, False, False)
            else:
                @pl.when(mate - gap >= 0)
                def _():
                    landed(item, mate - gap)
                    pass_on(item, mate - gap, False, False, False)

                @pl.when(mate + gap < member_n)
                def _():
                    landed(item, mate + gap)
                    pass_on(item, mate + gap, False, False, False)

        gap = 2 * (line - 1)

        @pl.when(mate - gap >= 0)
        def _():
            landed(item, mate - gap)
            pass_on(item, mate - gap, False, False, False)

        @pl.when(mate + gap < member_n)
        def _():
            landed(item, mate + gap)
            pass_on(item, mate + gap, False, False, False)

        if item == 0:
            feed()

    feed(nb)

    @pl.loop(0, nb)
    def _(block):
        crossing(block)

    keep_ints.wait()
    for hop_by in range(1, member_n):
        peer = lax.rem(me + hop_by, member_n)
        send(
            codes_hbm, ints_ref.at[peer], ints_send.at[hop_by], ints_recv.at[peer], peer, slab
        ).wait_recv()
    scalars = pltpu.make_async_copy(ints_ref, table_of_ints, local_sem.at[7])
    scalars.start()

    def source_of(place):
        return lax.rem(slab + space_n - 1 + place, space_n)

    load_window(0, 1, slab, win1_ref, values_ref, weights_ref, scratch1)
    for way in range(2):
        for member in range(member_n):
            side(member, way).wait_recv()
    for place in (near, far):
        load_window(0, place, source_of(place), win1_ref, values_ref, weights_ref, scratch1)
    scalars.wait()
    tiles_copy.wait()

    def choices(batch, owner, block):
        return [
            (
                table_of_ints[owner, batch, block * loc + l],
                table_of_ints[owner, batches + batch, block * loc + l],
            )
            for l in range(loc)
        ]

    def back_near(o):
        return send(
            win2_ref.at[1, o],
            win2_ref.at[far, o],
            back_send.at[o, 0],
            back_recv.at[o, 0],
            me,
            near_slab,
        )

    def back_far(o):
        part = pl.ds(pl.multiple_of(lane * quarter, 8), 3 * quarter)
        return send(
            win2_ref.at[1, o, part],
            win2_ref.at[near, o, part],
            back_send.at[o, 1],
            back_recv.at[o, 1],
            me,
            far_slab,
        )

    def rest(o, side_of):
        part = win2_ref.at[far, o, pl.ds(pl.multiple_of(side_of * 3 * quarter, 8), quarter)]
        return send(part, part, rest_send.at[o], rest_recv.at[o], mate, slab)

    def relay(o):
        back_far(o).wait_recv()
        rest(o, lane).start()

    @pl.loop(0, ob)
    def _(o):
        cell = cell_ref[1, 0, o]
        owner = cell // nb
        picks = choices(0, owner, cell - owner * nb)
        fresh = update(picks_ref[o], picks, tiles_ref, scratch1, acc_ref)
        win2_ref[1, o] = observe(fresh, table_ref[op_ref[1, 0, o]])
        back_near(o).start()
        back_far(o).start()

        @pl.when(o >= 2)
        def _():
            relay(o - 2)

    load_window(1, 1, slab, win2_ref, values_ref, weights_ref, scratch2)

    def first(block):
        stay(block).wait()
        for hop_by in range(1, member_n):
            peer = lax.rem(me + hop_by, member_n)
            send(
                states_ref.at[peer * nb + block],
                cells_ref.at[block, rows(peer)],
                in_send.at[block, hop_by],
                in_recv.at[block, peer],
                peer,
                slab,
            ).wait_recv()
        picks = choices(0, me, block)
        cells_ref[block] = update(cells_ref[block], picks, tiles_ref, scratch1, acc_ref)

    @pl.loop(0, ahead)
    def _(block):
        first(block)

        @pl.when(block < 2)
        def _():
            relay(ob - 2 + block)

    for o in range(ob):
        back_near(o).wait_recv()
    load_window(1, near, source_of(near), win2_ref, values_ref, weights_ref, scratch2)
    for o in range(ob):
        rest(o, 1 - lane).wait_recv()
    load_window(1, far, source_of(far), win2_ref, values_ref, weights_ref, scratch2)

    def give(block, hop_by):
        peer = lax.rem(me + hop_by, member_n)
        return send(
            cells_ref.at[block, rows(peer)],
            columns(out_ref, me * nb + block),
            out_send.at[block, hop_by],
            out_recv.at[block, me],
            peer,
            slab,
        )

    def keep(block):
        return pltpu.make_async_copy(
            cells_ref.at[block, rows(me)], columns(out_ref, me * nb + block), out_local.at[block]
        )

    @pl.loop(0, nb)
    def _(block):
        @pl.when((block >= 2) & (ahead - 2 + block < nb))
        def _():
            first(ahead - 2 + block)

        picks = choices(1, me, block)
        cells_ref[block] = update(cells_ref[block], picks, tiles_ref, scratch2, acc_ref)
        for hop_by in hops:
            give(block, hop_by).start()
        keep(block).start()

    for hop_by in range(1, member_n):
        give_ints(hop_by).wait_send()
    for member in range(member_n):
        spot, same = member // 2, lane == member % 2
        for way in range(2):
            side(member, way).wait_send()
        for item in range(2):
            @pl.when(same & (spot <= at) & (at < line - 1))
            def _():
                hop(item, member, 0, mate).wait_send()

            @pl.when(same & (spot >= at) & (at > 0))
            def _():
                hop(item, member, 1, mate).wait_send()

            @pl.when(same)
            def _():
                hop(item, member, 2, mate).wait_send()
    for o in range(ob):
        back_near(o).wait_send()
        back_far(o).wait_send()
        rest(o, lane).wait_send()

    @pl.loop(0, nb)
    def _(block):
        keep(block).wait()
        for hop_by in range(1, member_n):
            take(block, hop_by).wait_send()
            give(block, hop_by).wait_send()
            peer = lax.rem(me + hop_by, member_n)
            send(
                cells_ref.at[block, rows(peer)],
                columns(out_ref, peer * nb + block),
                out_send.at[block, hop_by],
                out_recv.at[block, peer],
                peer,
                slab,
            ).wait_recv()


def per_device(
    states, obs_values, obs_weights, obs_cell, op_select, op_table, loc_obs, loc_tile, loc_tiles
):
    member_n, space_n = lax.axis_size("member"), lax.axis_size("space")
    share, width = states.shape
    members = share * member_n
    ob = obs_cell.shape[2]
    batches, _, nb, loc = loc_obs.shape
    codes = jnp.stack([loc_obs, loc_tile]).reshape(2 * batches, nb * loc)
    f32, bf16, i32 = jnp.float32, jnp.bfloat16, jnp.int32
    hbm = pl.BlockSpec(memory_space=pltpu.HBM)
    dma = pltpu.SemaphoreType.DMA
    parts = [
        pltpu.VMEM((3 * ob, members, BLK), bf16),
        pltpu.VMEM((3 * ob, members, BLK), bf16),
        pltpu.VMEM((3 * ob, 1, BLK), f32),
        pltpu.VMEM((3 * ob, 1, BLK), f32),
    ]
    return pl.pallas_call(
        functools.partial(kernel, member_n, space_n, max(2, nb - 2)),
        out_shape=jax.ShapeDtypeStruct((share, width), f32),
        in_specs=[hbm] * 8,
        out_specs=pl.BlockSpec(memory_space=pl.ANY),
        scratch_shapes=[
            pltpu.SMEM(obs_cell.shape, i32),
            pltpu.SMEM(op_select.shape, i32),
            pltpu.VMEM(obs_values.shape, f32),
            pltpu.VMEM(obs_weights.shape, f32),
            pltpu.VMEM(op_table.shape, f32),
            pltpu.VMEM(loc_tiles.shape, f32),
            pltpu.SMEM((member_n,) + codes.shape, i32),
            pltpu.VMEM((member_n,) + codes.shape, i32),
            pltpu.VMEM((width // BLK, share, BLK), f32),
            pltpu.VMEM((nb, members, BLK), f32),
            pltpu.VMEM((ob, members, BLK), f32),
            pltpu.VMEM((3, ob, members, BLK), f32),
            pltpu.VMEM((3, ob, members, BLK), f32),
            pltpu.VMEM((members, BLK), f32),
        ] + parts + parts + [
            dma((width // BLK,)),
            dma((8,)),
            dma((member_n,)),
            dma((member_n,)),
            dma((2, member_n, 3)),
            dma((2, member_n)),
            dma((member_n, 2)),
            dma((member_n, 2)),
            dma((nb, member_n)),
            dma((nb, member_n)),
            dma((nb,)),
            dma((ob, 2)),
            dma((ob, 2)),
            dma((ob,)),
            dma((ob,)),
            dma((nb, member_n)),
            dma((nb, member_n)),
            dma((nb,)),
        ],
        compiler_params=pltpu.CompilerParams(
            vmem_limit_bytes=58 * 1024 * 1024, collective_id=0, has_side_effects=True
        ),
    )(obs_cell, op_select, obs_values, obs_weights, op_table, codes, states, loc_tiles)


def solution(mesh):
    placed = (
        P("member", "space"),
        P(),
        P(),
        P(None, "space", None),
        P(None, "space", None),
        P(),
        P(None, "space", "member", None),
        P(None, "space", "member", None),
        P(),
    )
    return jax.shard_map(
        per_device, mesh=mesh, in_specs=placed, out_specs=P("member", "space"), check_vma=False
    )
```

```python
import functools

import jax
import jax.numpy as jnp
from jax import lax
from jax.experimental import pallas as pl
from jax.experimental.pallas import tpu as pltpu
from jax.sharding import PartitionSpec as P

BLK = 128
NT_DIMS = (((1,), (1,)), ((), ()))


def split(x):
    hi = x.astype(jnp.bfloat16)
    lo = (x - hi.astype(jnp.float32)).astype(jnp.bfloat16)
    return hi, lo


def dot(a, b):
    return jnp.dot(a, b, preferred_element_type=jnp.float32)


def dot_nt(a, b):
    return lax.dot_general(a, b, NT_DIMS, preferred_element_type=jnp.float32)


def observe(block, operator):
    hi, lo = split(block)
    op_hi, op_lo = split(operator)
    part = dot_nt(hi, jnp.concatenate([op_hi, op_lo], axis=0))
    return part[:, :BLK] + part[:, BLK:] + dot_nt(lo, op_hi)


def send(src, dst, send_sem, recv_sem, member, space):
    return pltpu.make_async_remote_copy(
        src_ref=src,
        dst_ref=dst,
        send_sem=send_sem,
        recv_sem=recv_sem,
        device_id=(member, space),
        device_id_type=pl.DeviceIdType.MESH,
    )


def columns(ref, block):
    return ref.at[:, pl.ds(pl.multiple_of(block * BLK, BLK), BLK)]


def load_block(batch, place, o, source, window_ref, values_ref, weights_ref, scratch):
    hi_ref, lo_ref, d_ref, w_ref = scratch
    _, ob, members, _ = window_ref.shape
    j = place * ob + o
    at = pl.ds(pl.multiple_of((source * ob + o) * BLK, BLK), BLK)
    weight = weights_ref[batch:batch + 1, at]
    block = window_ref[place, o]
    mean = jnp.sum(block, axis=0, keepdims=True) * (1.0 / members)
    hi, lo = split(block - mean)
    hi_ref[j] = hi
    lo_ref[j] = lo
    w_ref[j] = weight
    d_ref[j] = weight * (values_ref[batch:batch + 1, at] - mean)


def load_window(batch, place, source, window_ref, *rest):
    for o in range(window_ref.shape[1]):
        load_block(batch, place, o, source, window_ref, *rest)


def gains(cell, picks, tiles_ref, scratch, gain_ref):
    hi_ref, lo_ref, d_ref, w_ref = scratch
    members = cell.shape[0]
    mean = jnp.sum(cell, axis=0, keepdims=True) * (1.0 / members)
    hi, lo = split(jnp.transpose(cell - mean))
    both = jnp.concatenate([hi, lo], axis=0)
    ones = []
    for pair in range(len(picks) // 2):
        (first, tile_a), (second, tile_b) = picks[2 * pair], picks[2 * pair + 1]
        obs_hi = jnp.concatenate([hi_ref[first], hi_ref[second]], axis=1)
        obs_lo = jnp.concatenate([lo_ref[first], lo_ref[second]], axis=1)
        part = dot(both, obs_hi)
        cov = part[:BLK] + part[BLK:] + dot(hi, obs_lo)
        tile = jnp.concatenate([tiles_ref[tile_a], tiles_ref[tile_b]], axis=1)
        gain = tile * (cov * (1.0 / (members - 1)))
        d = jnp.concatenate([d_ref[first], d_ref[second]], axis=1)
        w = jnp.concatenate([w_ref[first], w_ref[second]], axis=1)
        ones.append(jnp.sum(gain * d, axis=1, keepdims=True))
        gain_hi, gain_lo = split(gain * (-0.5 * w))
        gain_ref[:BLK, 2 * pair * BLK:2 * (pair + 1) * BLK] = gain_hi
        gain_ref[BLK:, 2 * pair * BLK:2 * (pair + 1) * BLK] = gain_lo
    shift = functools.reduce(jnp.add, ones)
    return jnp.transpose(jnp.broadcast_to(shift, (BLK, BLK)))[:1]


def moved(part, at, picks, row, scratch, gain_ref):
    hi_ref, lo_ref = scratch[:2]
    obs_hi = jnp.concatenate([hi_ref[j, at] for j, _ in picks], axis=1)
    obs_lo = jnp.concatenate([lo_ref[j, at] for j, _ in picks], axis=1)
    step = dot_nt(obs_hi, gain_ref[...])
    return part + (step[:, :BLK] + step[:, BLK:] + dot_nt(obs_lo, gain_ref[:BLK]) + row)


def kernel(member_n, space_n, ahead, *refs):
    sources, states_hbm, tiles_hbm, out_ref, refs = refs[:6], refs[6], refs[7], refs[8], refs[9:]
    copies, (tiles_ref, table_of_ints, ints_ref), refs = refs[:5], refs[5:8], refs[8:]
    cell_ref, op_ref, values_ref, weights_ref, table_ref = copies
    states_ref, cells_ref, picks_ref, win1_ref, win2_ref, gain_ref = refs[:6]
    scratch1, scratch2, refs = refs[6:10], refs[10:14], refs[14:]
    load_sem, local_sem, ints_send, ints_recv, hop_send, hop_recv, halo_send, halo_recv = refs[:8]
    in_send, in_recv, in_local, back_send, back_recv, rest_send, rest_recv = refs[8:15]
    far_send, far_recv, out_send, out_recv, out_local = refs[15:]
    codes_hbm = sources[5]

    nb, members, _ = cells_ref.shape
    ob = picks_ref.shape[0]
    share = states_ref.shape[1]
    batches = cell_ref.shape[0]
    loc = codes_hbm.shape[1] // nb
    me = lax.axis_index("member")
    slab = lax.axis_index("space")
    after = lax.rem(slab + 1, space_n)
    before = lax.rem(slab + space_n - 1, space_n)
    line = member_n // 2
    at, lane = me // 2, lax.rem(me, 2)
    mate = at * 2 + 1 - lane
    odd = lax.rem(slab, 2)
    near, far = 2 * (1 - odd), 2 * odd
    near_slab = slab + 1 - 2 * odd
    far_slab = lax.rem(slab + space_n - 1 + 2 * odd, space_n)
    quarter = members // 4

    barrier = pltpu.get_barrier_semaphore()

    def greet(member, space):
        pl.semaphore_signal(
            barrier, inc=1, device_id=(member, space), device_id_type=pl.DeviceIdType.MESH
        )

    greet(me, after)
    greet(me, before)
    for hop_by in range(1, member_n):
        greet(lax.rem(me + hop_by, member_n), slab)

    small = [
        pltpu.make_async_copy(sources[i], copies[i], local_sem.at[i]) for i in range(len(copies))
    ]
    for copy in small:
        copy.start()

    def load(block):
        return pltpu.make_async_copy(
            columns(states_hbm, block), states_ref.at[block], load_sem.at[block]
        )

    @pl.loop(0, member_n * nb)
    def _(block):
        load(block).start()

    tiles_copy = pltpu.make_async_copy(tiles_hbm, tiles_ref, local_sem.at[5])
    tiles_copy.start()
    keep_ints = pltpu.make_async_copy(codes_hbm, ints_ref.at[me], local_sem.at[6])
    keep_ints.start()

    def rows(member):
        return pl.ds(pl.multiple_of(member * share, 8), share)

    for copy in small:
        copy.wait()

    @pl.loop(0, member_n * nb)
    def _(block):
        load(block).wait()

    own_ref = win1_ref.at[1]
    for o in range(ob):
        own_ref[o, rows(me)] = observe(states_ref[cell_ref[0, 0, o]], table_ref[op_ref[0, 0, o]])
    for o in range(ob):
        picks_ref[o, rows(me)] = states_ref[cell_ref[1, 0, o]]
    pl.semaphore_wait(barrier, member_n + 1)

    def hop(item, member, way, target):
        part = (own_ref, picks_ref)[item].at[:, rows(member)]
        return send(
            part, part, hop_send.at[item, member, way], hop_recv.at[item, member], target, slab
        )

    def side(member, way):
        return send(
            own_ref.at[:, rows(member)],
            win1_ref.at[2 * way, :, rows(member)],
            halo_send.at[member, way],
            halo_recv.at[member, way],
            me,
            (after, before)[way],
        )

    def pass_on(item, member, up, down, across):
        if up:
            @pl.when(at < line - 1)
            def _():
                hop(item, member, 0, me + 2).start()

        if down:
            @pl.when(at > 0)
            def _():
                hop(item, member, 1, me - 2).start()

        if across:
            hop(item, member, 2, mate).start()
        if item == 0:
            side(member, 0).start()
            side(member, 1).start()

    def landed(item, member):
        hop(item, member, 2, mate).wait_recv()

    def take(block, hop_by):
        peer = lax.rem(me + hop_by, member_n)
        return send(
            states_ref.at[peer * nb + block],
            cells_ref.at[block, rows(me)],
            in_send.at[block, hop_by],
            in_recv.at[block, me],
            peer,
            slab,
        )

    def stay(block):
        return pltpu.make_async_copy(
            states_ref.at[me * nb + block], cells_ref.at[block, rows(me)], in_local.at[block]
        )

    hops = sorted(range(1, member_n), key=lambda k: (abs(k - line), k))

    def straight(block):
        for hop_by in hops:
            if hop_by % 2 == 0:
                take(block, hop_by).start()
        stay(block).start()

    def crossing(block):
        for hop_by in hops:
            if hop_by % 2 == 1:
                take(block, hop_by).start()

    waiting = list(range(nb))

    def feed(count=1):
        for _ in range(min(count, len(waiting))):
            straight(waiting.pop(0))

    def give_ints(hop_by):
        peer = lax.rem(me + hop_by, member_n)
        return send(
            codes_hbm, ints_ref.at[me], ints_send.at[hop_by], ints_recv.at[me], peer, slab
        )

    pass_on(0, me, True, True, True)
    for hop_by in range(1, member_n):
        give_ints(hop_by).start()
    pass_on(1, me, True, True, True)
    feed()

    for item in range(2):
        for step in range(1, line):
            low, high = me - 2 * step, me + 2 * step

            @pl.when(low >= 0)
            def _():
                landed(item, low)
                pass_on(item, low, True, False, True)

            @pl.when(high < member_n)
            def _():
                landed(item, high)
                pass_on(item, high, False, True, True)

            if step == 1:
                feed()
            gap = 2 * (step - 1)
            if gap == 0:
                landed(item, mate)
                pass_on(item, mate, False, False, False)
            else:
                @pl.when(mate - gap >= 0)
                def _():
                    landed(item, mate - gap)
                    pass_on(item, mate - gap, False, False, False)

                @pl.when(mate + gap < member_n)
                def _():
                    landed(item, mate + gap)
                    pass_on(item, mate + gap, False, False, False)

        gap = 2 * (line - 1)

        @pl.when(mate - gap >= 0)
        def _():
            landed(item, mate - gap)
            pass_on(item, mate - gap, False, False, False)

        @pl.when(mate + gap < member_n)
        def _():
            landed(item, mate + gap)
            pass_on(item, mate + gap, False, False, False)

        if item == 0:
            feed()

    feed(nb)

    @pl.loop(0, nb)
    def _(block):
        crossing(block)

    keep_ints.wait()
    for hop_by in range(1, member_n):
        peer = lax.rem(me + hop_by, member_n)
        send(
            codes_hbm, ints_ref.at[peer], ints_send.at[hop_by], ints_recv.at[peer], peer, slab
        ).wait_recv()
    scalars = pltpu.make_async_copy(ints_ref, table_of_ints, local_sem.at[7])
    scalars.start()

    def source_of(place):
        return lax.rem(slab + space_n - 1 + place, space_n)

    load_window(0, 1, slab, win1_ref, values_ref, weights_ref, scratch1)
    for way in range(2):
        for member in range(member_n):
            side(member, way).wait_recv()
    for place in (near, far):
        load_window(0, place, source_of(place), win1_ref, values_ref, weights_ref, scratch1)
    scalars.wait()
    tiles_copy.wait()

    def choices(batch, owner, block):
        return [
            (
                table_of_ints[owner, batch, block * loc + l],
                table_of_ints[owner, batches + batch, block * loc + l],
            )
            for l in range(loc)
        ]

    def back_near(o):
        return send(
            win2_ref.at[1, o],
            win2_ref.at[far, o],
            back_send.at[o],
            back_recv.at[o],
            me,
            near_slab,
        )

    def rows_of(q):
        return pl.ds(pl.multiple_of(q * quarter, 16), quarter)

    def back_far(o, q):
        return send(
            win2_ref.at[1, o, rows_of(q)],
            win2_ref.at[near, o, rows_of(q)],
            far_send.at[o, q],
            far_recv.at[o, q],
            me,
            far_slab,
        )

    def rest(o, side_of):
        part = win2_ref.at[far, o, rows_of(side_of * 3)]
        return send(part, part, rest_send.at[o], rest_recv.at[o], mate, slab)

    def relay(o):
        back_far(o, lane * 3).wait_recv()
        rest(o, lane).start()

    @pl.loop(0, ob)
    def _(o):
        cell = cell_ref[1, 0, o]
        owner = cell // nb
        picks = choices(0, owner, cell - owner * nb)
        row = gains(picks_ref[o], picks, tiles_ref, scratch1, gain_ref)
        operator = table_ref[op_ref[1, 0, o]]

        @pl.loop(0, 4)
        def _(turn):
            q = turn + lane * (3 - 2 * turn)
            at_q = rows_of(q)
            fresh = moved(picks_ref[o, at_q], at_q, picks, row, scratch1, gain_ref)
            win2_ref[1, o, at_q] = observe(fresh, operator)

            @pl.when(turn < 3)
            def _():
                back_far(o, q).start()

        back_near(o).start()

        @pl.when(o >= 2)
        def _():
            relay(o - 2)

    load_window(1, 1, slab, win2_ref, values_ref, weights_ref, scratch2)

    def first(block):
        stay(block).wait()
        for hop_by in range(1, member_n):
            peer = lax.rem(me + hop_by, member_n)
            send(
                states_ref.at[peer * nb + block],
                cells_ref.at[block, rows(peer)],
                in_send.at[block, hop_by],
                in_recv.at[block, peer],
                peer,
                slab,
            ).wait_recv()
        picks = choices(0, me, block)
        row = gains(cells_ref[block], picks, tiles_ref, scratch1, gain_ref)

        @pl.loop(0, 4)
        def _(q):
            at_q = rows_of(q)
            part = cells_ref[block, at_q]
            cells_ref[block, at_q] = moved(part, at_q, picks, row, scratch1, gain_ref)

    @pl.loop(0, ahead)
    def _(block):
        first(block)

        @pl.when(block < 2)
        def _():
            relay(ob - 2 + block)

    for o in range(ob):
        back_near(o).wait_recv()
    load_window(1, near, source_of(near), win2_ref, values_ref, weights_ref, scratch2)
    for o in range(ob):
        back_far(o, 1).wait_recv()
        back_far(o, 2).wait_recv()
        rest(o, 1 - lane).wait_recv()
        load_block(1, far, o, source_of(far), win2_ref, values_ref, weights_ref, scratch2)

    def give(block, peer):
        return send(
            cells_ref.at[block, rows(peer)],
            columns(out_ref, me * nb + block),
            out_send.at[block, peer],
            out_recv.at[block, me],
            peer,
            slab,
        )

    def keep(block):
        return pltpu.make_async_copy(
            cells_ref.at[block, rows(me)], columns(out_ref, me * nb + block), out_local.at[block]
        )

    opposite = jnp.where(at < line // 2, 2, 0)
    group = member_n // 4

    @pl.loop(0, nb)
    def _(block):
        @pl.when((block >= 2) & (ahead - 2 + block < nb))
        def _():
            first(ahead - 2 + block)

        picks = choices(1, me, block)
        row = gains(cells_ref[block], picks, tiles_ref, scratch2, gain_ref)

        @pl.loop(0, 4)
        def _(turn):
            q = lax.rem(turn + opposite, 4)
            at_q = rows_of(q)
            part = cells_ref[block, at_q]
            cells_ref[block, at_q] = moved(part, at_q, picks, row, scratch2, gain_ref)
            for k in range(group):
                peer = q * group + k

                @pl.when(peer != me)
                def _():
                    give(block, peer).start()

                @pl.when(peer == me)
                def _():
                    keep(block).start()

    for hop_by in range(1, member_n):
        give_ints(hop_by).wait_send()
    for member in range(member_n):
        spot, same = member // 2, lane == member % 2
        for way in range(2):
            side(member, way).wait_send()
        for item in range(2):
            @pl.when(same & (spot <= at) & (at < line - 1))
            def _():
                hop(item, member, 0, mate).wait_send()

            @pl.when(same & (spot >= at) & (at > 0))
            def _():
                hop(item, member, 1, mate).wait_send()

            @pl.when(same)
            def _():
                hop(item, member, 2, mate).wait_send()
    for o in range(ob):
        back_near(o).wait_send()
        for turn in range(3):
            back_far(o, turn + lane * (3 - 2 * turn)).wait_send()
        rest(o, lane).wait_send()

    @pl.loop(0, nb)
    def _(block):
        keep(block).wait()
        for hop_by in range(1, member_n):
            take(block, hop_by).wait_send()
            peer = lax.rem(me + hop_by, member_n)
            give(block, peer).wait_send()
            send(
                cells_ref.at[block, rows(peer)],
                columns(out_ref, peer * nb + block),
                out_send.at[block, peer],
                out_recv.at[block, peer],
                peer,
                slab,
            ).wait_recv()


def per_device(
    states, obs_values, obs_weights, obs_cell, op_select, op_table, loc_obs, loc_tile, loc_tiles
):
    member_n, space_n = lax.axis_size("member"), lax.axis_size("space")
    share, width = states.shape
    members = share * member_n
    ob = obs_cell.shape[2]
    batches, _, nb, loc = loc_obs.shape
    codes = jnp.stack([loc_obs, loc_tile]).reshape(2 * batches, nb * loc)
    f32, bf16, i32 = jnp.float32, jnp.bfloat16, jnp.int32
    hbm = pl.BlockSpec(memory_space=pltpu.HBM)
    dma = pltpu.SemaphoreType.DMA
    parts = [
        pltpu.VMEM((3 * ob, members, BLK), bf16),
        pltpu.VMEM((3 * ob, members, BLK), bf16),
        pltpu.VMEM((3 * ob, 1, BLK), f32),
        pltpu.VMEM((3 * ob, 1, BLK), f32),
    ]
    return pl.pallas_call(
        functools.partial(kernel, member_n, space_n, max(2, nb - 3)),
        out_shape=jax.ShapeDtypeStruct((share, width), f32),
        in_specs=[hbm] * 8,
        out_specs=pl.BlockSpec(memory_space=pl.ANY),
        scratch_shapes=[
            pltpu.SMEM(obs_cell.shape, i32),
            pltpu.SMEM(op_select.shape, i32),
            pltpu.VMEM(obs_values.shape, f32),
            pltpu.VMEM(obs_weights.shape, f32),
            pltpu.VMEM(op_table.shape, f32),
            pltpu.VMEM(loc_tiles.shape, f32),
            pltpu.SMEM((member_n,) + codes.shape, i32),
            pltpu.VMEM((member_n,) + codes.shape, i32),
            pltpu.VMEM((width // BLK, share, BLK), f32),
            pltpu.VMEM((nb, members, BLK), f32),
            pltpu.VMEM((ob, members, BLK), f32),
            pltpu.VMEM((3, ob, members, BLK), f32),
            pltpu.VMEM((3, ob, members, BLK), f32),
            pltpu.VMEM((2 * BLK, loc * BLK), bf16),
        ] + parts + parts + [
            dma((width // BLK,)),
            dma((8,)),
            dma((member_n,)),
            dma((member_n,)),
            dma((2, member_n, 3)),
            dma((2, member_n)),
            dma((member_n, 2)),
            dma((member_n, 2)),
            dma((nb, member_n)),
            dma((nb, member_n)),
            dma((nb,)),
            dma((ob,)),
            dma((ob,)),
            dma((ob,)),
            dma((ob,)),
            dma((ob, 4)),
            dma((ob, 4)),
            dma((nb, member_n)),
            dma((nb, member_n)),
            dma((nb,)),
        ],
        compiler_params=pltpu.CompilerParams(
            vmem_limit_bytes=58 * 1024 * 1024, collective_id=0, has_side_effects=True
        ),
    )(obs_cell, op_select, obs_values, obs_weights, op_table, codes, states, loc_tiles)


def solution(mesh):
    placed = (
        P("member", "space"),
        P(),
        P(),
        P(None, "space", None),
        P(None, "space", None),
        P(),
        P(None, "space", "member", None),
        P(None, "space", "member", None),
        P(),
    )
    return jax.shard_map(
        per_device, mesh=mesh, in_specs=placed, out_specs=P("member", "space"), check_vma=False
    )
```

```python
import functools

import jax
import jax.numpy as jnp
from jax import lax
from jax.experimental import pallas as pl
from jax.experimental.pallas import tpu as pltpu
from jax.sharding import PartitionSpec as P

BLK = 128
NT_DIMS = (((1,), (1,)), ((), ()))


def split(x):
    hi = x.astype(jnp.bfloat16)
    lo = (x - hi.astype(jnp.float32)).astype(jnp.bfloat16)
    return hi, lo


def dot(a, b):
    return jnp.dot(a, b, preferred_element_type=jnp.float32)


def dot_nt(a, b):
    return lax.dot_general(a, b, NT_DIMS, preferred_element_type=jnp.float32)


def observe(block, operator):
    hi, lo = split(block)
    op_hi, op_lo = split(operator)
    part = dot_nt(hi, jnp.concatenate([op_hi, op_lo], axis=0))
    return part[:, :BLK] + part[:, BLK:] + dot_nt(lo, op_hi)


def send(src, dst, send_sem, recv_sem, member, space):
    return pltpu.make_async_remote_copy(
        src_ref=src,
        dst_ref=dst,
        send_sem=send_sem,
        recv_sem=recv_sem,
        device_id=(member, space),
        device_id_type=pl.DeviceIdType.MESH,
    )


def columns(ref, block):
    return ref.at[:, pl.ds(pl.multiple_of(block * BLK, BLK), BLK)]


def load_block(batch, place, o, source, window_ref, values_ref, weights_ref, scratch):
    hi_ref, lo_ref, d_ref, w_ref = scratch
    _, ob, members, _ = window_ref.shape
    j = place * ob + o
    at = pl.ds(pl.multiple_of((source * ob + o) * BLK, BLK), BLK)
    weight = weights_ref[batch:batch + 1, at]
    block = window_ref[place, o]
    mean = jnp.sum(block, axis=0, keepdims=True) * (1.0 / members)
    hi, lo = split(block - mean)
    hi_ref[j] = hi
    lo_ref[j] = lo
    w_ref[j] = weight
    d_ref[j] = weight * (values_ref[batch:batch + 1, at] - mean)


def load_window(batch, place, source, window_ref, *rest):
    for o in range(window_ref.shape[1]):
        load_block(batch, place, o, source, window_ref, *rest)


def gains(cell, picks, tiles_ref, scratch, gain_ref):
    hi_ref, lo_ref, d_ref, w_ref = scratch
    members = cell.shape[0]
    mean = jnp.sum(cell, axis=0, keepdims=True) * (1.0 / members)
    hi, lo = split(jnp.transpose(cell - mean))
    both = jnp.concatenate([hi, lo], axis=0)
    ones = []
    for pair in range(len(picks) // 2):
        (first, tile_a), (second, tile_b) = picks[2 * pair], picks[2 * pair + 1]
        obs_hi = jnp.concatenate([hi_ref[first], hi_ref[second]], axis=1)
        obs_lo = jnp.concatenate([lo_ref[first], lo_ref[second]], axis=1)
        part = dot(both, obs_hi)
        cov = part[:BLK] + part[BLK:] + dot(hi, obs_lo)
        tile = jnp.concatenate([tiles_ref[tile_a], tiles_ref[tile_b]], axis=1)
        gain = tile * (cov * (1.0 / (members - 1)))
        d = jnp.concatenate([d_ref[first], d_ref[second]], axis=1)
        w = jnp.concatenate([w_ref[first], w_ref[second]], axis=1)
        ones.append(jnp.sum(gain * d, axis=1, keepdims=True))
        gain_hi, gain_lo = split(gain * (-0.5 * w))
        gain_ref[:BLK, 2 * pair * BLK:2 * (pair + 1) * BLK] = gain_hi
        gain_ref[BLK:, 2 * pair * BLK:2 * (pair + 1) * BLK] = gain_lo
    shift = functools.reduce(jnp.add, ones)
    return jnp.transpose(jnp.broadcast_to(shift, (BLK, BLK)))[:1]


def moved(part, at, picks, row, scratch, gain_ref):
    hi_ref, lo_ref = scratch[:2]
    obs_hi = jnp.concatenate([hi_ref[j, at] for j, _ in picks], axis=1)
    obs_lo = jnp.concatenate([lo_ref[j, at] for j, _ in picks], axis=1)
    step = dot_nt(obs_hi, gain_ref[...])
    return part + (step[:, :BLK] + step[:, BLK:] + dot_nt(obs_lo, gain_ref[:BLK]) + row)


def kernel(member_n, space_n, ahead, *refs):
    sources, states_hbm, tiles_hbm, out_ref, refs = refs[:6], refs[6], refs[7], refs[8], refs[9:]
    copies, (tiles_ref, table_of_ints, ints_ref), refs = refs[:5], refs[5:8], refs[8:]
    cell_ref, op_ref, values_ref, weights_ref, table_ref = copies
    states_ref, cells_ref, picks_ref, win1_ref, win2_ref, gain_ref = refs[:6]
    scratch1, scratch2, refs = refs[6:10], refs[10:14], refs[14:]
    load_sem, local_sem, ints_send, ints_recv, hop_send, hop_recv, halo_send, halo_recv = refs[:8]
    in_send, in_recv, in_local, back_send, back_recv, rest_send, rest_recv = refs[8:15]
    far_send, far_recv, out_send, out_recv, out_local = refs[15:]
    codes_hbm = sources[5]

    slots, members, _ = cells_ref.shape
    nb = slots - 1
    ob = picks_ref.shape[0]
    share = states_ref.shape[1]
    batches = cell_ref.shape[0]
    loc = codes_hbm.shape[1] // nb
    me = lax.axis_index("member")
    slab = lax.axis_index("space")
    after = lax.rem(slab + 1, space_n)
    before = lax.rem(slab + space_n - 1, space_n)
    line = member_n // 2
    at, lane = me // 2, lax.rem(me, 2)
    mate = at * 2 + 1 - lane
    odd = lax.rem(slab, 2)
    near, far = 2 * (1 - odd), 2 * odd
    near_slab = slab + 1 - 2 * odd
    far_slab = lax.rem(slab + space_n - 1 + 2 * odd, space_n)
    quarter = members // 4
    half = member_n // 2
    partner = lax.rem(me + half, member_n)

    def block_of(member, slot):
        other = lax.rem(member + half, member_n)
        return jnp.where(slot < nb, member * nb + slot, other * nb + nb - 1)

    def reached(member, slot):
        return (slot < nb - 1) | (member // half == me // half)

    barrier = pltpu.get_barrier_semaphore()

    def greet(member, space):
        pl.semaphore_signal(
            barrier, inc=1, device_id=(member, space), device_id_type=pl.DeviceIdType.MESH
        )

    greet(me, after)
    greet(me, before)
    for hop_by in range(1, member_n):
        greet(lax.rem(me + hop_by, member_n), slab)

    small = [
        pltpu.make_async_copy(sources[i], copies[i], local_sem.at[i]) for i in range(len(copies))
    ]
    for copy in small:
        copy.start()

    def load(block):
        return pltpu.make_async_copy(
            columns(states_hbm, block), states_ref.at[block], load_sem.at[block]
        )

    @pl.loop(0, member_n * nb)
    def _(block):
        load(block).start()

    tiles_copy = pltpu.make_async_copy(tiles_hbm, tiles_ref, local_sem.at[5])
    tiles_copy.start()
    keep_ints = pltpu.make_async_copy(codes_hbm, ints_ref.at[me], local_sem.at[6])
    keep_ints.start()

    def rows(member):
        return pl.ds(pl.multiple_of(member * share, 8), share)

    for copy in small:
        copy.wait()

    @pl.loop(0, member_n * nb)
    def _(block):
        load(block).wait()

    own_ref = win1_ref.at[1]
    for o in range(ob):
        own_ref[o, rows(me)] = observe(states_ref[cell_ref[0, 0, o]], table_ref[op_ref[0, 0, o]])
    for o in range(ob):
        picks_ref[o, rows(me)] = states_ref[cell_ref[1, 0, o]]
    pl.semaphore_wait(barrier, member_n + 1)

    def hop(item, member, way, target):
        part = (own_ref, picks_ref)[item].at[:, rows(member)]
        return send(
            part, part, hop_send.at[item, member, way], hop_recv.at[item, member], target, slab
        )

    def side(member, way):
        return send(
            own_ref.at[:, rows(member)],
            win1_ref.at[2 * way, :, rows(member)],
            halo_send.at[member, way],
            halo_recv.at[member, way],
            me,
            (after, before)[way],
        )

    def pass_on(item, member, up, down, across):
        if up:
            @pl.when(at < line - 1)
            def _():
                hop(item, member, 0, me + 2).start()

        if down:
            @pl.when(at > 0)
            def _():
                hop(item, member, 1, me - 2).start()

        if across:
            hop(item, member, 2, mate).start()
        if item == 0:
            side(member, 0).start()
            side(member, 1).start()

    def landed(item, member):
        hop(item, member, 2, mate).wait_recv()

    def take(block, hop_by):
        peer = lax.rem(me + hop_by, member_n)
        return send(
            states_ref.at[block_of(peer, block)],
            cells_ref.at[block, rows(me)],
            in_send.at[block, hop_by],
            in_recv.at[block, me],
            peer,
            slab,
        )

    def stay(block):
        return pltpu.make_async_copy(
            states_ref.at[block_of(me, block)], cells_ref.at[block, rows(me)], in_local.at[block]
        )

    hops = sorted(range(1, member_n), key=lambda k: (abs(k - line), k))

    def straight(block):
        for hop_by in hops:
            if hop_by % 2 == 0:
                take(block, hop_by).start()
        stay(block).start()

    def crossing(block):
        for hop_by in hops:
            if hop_by % 2 == 1:
                take(block, hop_by).start()

    waiting = list(range(slots))

    def feed(count=1):
        for _ in range(min(count, len(waiting))):
            straight(waiting.pop(0))

    def give_ints(hop_by):
        peer = lax.rem(me + hop_by, member_n)
        return send(
            codes_hbm, ints_ref.at[me], ints_send.at[hop_by], ints_recv.at[me], peer, slab
        )

    pass_on(0, me, True, True, True)
    for hop_by in range(1, member_n):
        give_ints(hop_by).start()
    pass_on(1, me, True, True, True)
    feed()

    for item in range(2):
        for step in range(1, line):
            low, high = me - 2 * step, me + 2 * step

            @pl.when(low >= 0)
            def _():
                landed(item, low)
                pass_on(item, low, True, False, True)

            @pl.when(high < member_n)
            def _():
                landed(item, high)
                pass_on(item, high, False, True, True)

            if step == 1:
                feed()
            gap = 2 * (step - 1)
            if gap == 0:
                landed(item, mate)
                pass_on(item, mate, False, False, False)
            else:
                @pl.when(mate - gap >= 0)
                def _():
                    landed(item, mate - gap)
                    pass_on(item, mate - gap, False, False, False)

                @pl.when(mate + gap < member_n)
                def _():
                    landed(item, mate + gap)
                    pass_on(item, mate + gap, False, False, False)

        gap = 2 * (line - 1)

        @pl.when(mate - gap >= 0)
        def _():
            landed(item, mate - gap)
            pass_on(item, mate - gap, False, False, False)

        @pl.when(mate + gap < member_n)
        def _():
            landed(item, mate + gap)
            pass_on(item, mate + gap, False, False, False)

        if item == 0:
            feed()

    feed(slots)

    @pl.loop(0, slots)
    def _(block):
        crossing(block)

    keep_ints.wait()
    for hop_by in range(1, member_n):
        peer = lax.rem(me + hop_by, member_n)
        send(
            codes_hbm, ints_ref.at[peer], ints_send.at[hop_by], ints_recv.at[peer], peer, slab
        ).wait_recv()
    scalars = pltpu.make_async_copy(ints_ref, table_of_ints, local_sem.at[7])
    scalars.start()

    def source_of(place):
        return lax.rem(slab + space_n - 1 + place, space_n)

    load_window(0, 1, slab, win1_ref, values_ref, weights_ref, scratch1)
    for way in range(2):
        for member in range(member_n):
            side(member, way).wait_recv()
    for place in (near, far):
        load_window(0, place, source_of(place), win1_ref, values_ref, weights_ref, scratch1)
    scalars.wait()
    tiles_copy.wait()

    def choices_of(batch, slot):
        owner = jnp.where(slot < nb, me, partner)
        return choices(batch, owner, jnp.where(slot < nb, slot, nb - 1))

    def choices(batch, owner, block):
        return [
            (
                table_of_ints[owner, batch, block * loc + l],
                table_of_ints[owner, batches + batch, block * loc + l],
            )
            for l in range(loc)
        ]

    def back_near(o):
        return send(
            win2_ref.at[1, o],
            win2_ref.at[far, o],
            back_send.at[o],
            back_recv.at[o],
            me,
            near_slab,
        )

    def rows_of(q):
        return pl.ds(pl.multiple_of(q * quarter, 16), quarter)

    def back_far(o, q):
        return send(
            win2_ref.at[1, o, rows_of(q)],
            win2_ref.at[near, o, rows_of(q)],
            far_send.at[o, q],
            far_recv.at[o, q],
            me,
            far_slab,
        )

    def rest(o, side_of):
        part = win2_ref.at[far, o, rows_of(side_of * 3)]
        return send(part, part, rest_send.at[o], rest_recv.at[o], mate, slab)

    def relay(o):
        back_far(o, lane * 3).wait_recv()
        rest(o, lane).start()

    @pl.loop(0, ob)
    def _(o):
        cell = cell_ref[1, 0, o]
        owner = cell // nb
        picks = choices(0, owner, cell - owner * nb)
        row = gains(picks_ref[o], picks, tiles_ref, scratch1, gain_ref)
        operator = table_ref[op_ref[1, 0, o]]

        @pl.loop(0, 4)
        def _(turn):
            q = turn + lane * (3 - 2 * turn)
            at_q = rows_of(q)
            fresh = moved(picks_ref[o, at_q], at_q, picks, row, scratch1, gain_ref)
            win2_ref[1, o, at_q] = observe(fresh, operator)

            back_far(o, q).start()

        back_near(o).start()


    load_window(1, 1, slab, win2_ref, values_ref, weights_ref, scratch2)

    def first(block):
        stay(block).wait()
        for hop_by in range(1, member_n):
            peer = lax.rem(me + hop_by, member_n)
            send(
                states_ref.at[block_of(peer, block)],
                cells_ref.at[block, rows(peer)],
                in_send.at[block, hop_by],
                in_recv.at[block, peer],
                peer,
                slab,
            ).wait_recv()
        picks = choices_of(0, block)
        row = gains(cells_ref[block], picks, tiles_ref, scratch1, gain_ref)

        @pl.loop(0, 4)
        def _(q):
            at_q = rows_of(q)
            part = cells_ref[block, at_q]
            cells_ref[block, at_q] = moved(part, at_q, picks, row, scratch1, gain_ref)

    @pl.loop(0, ahead)
    def _(block):
        first(block)


    for o in range(ob):
        back_near(o).wait_recv()
    load_window(1, near, source_of(near), win2_ref, values_ref, weights_ref, scratch2)
    for o in range(ob):
        for q in range(4):
            back_far(o, q).wait_recv()
        load_block(1, far, o, source_of(far), win2_ref, values_ref, weights_ref, scratch2)

    def give(block, peer):
        return send(
            cells_ref.at[block, rows(peer)],
            columns(out_ref, block_of(me, block)),
            out_send.at[block, peer],
            out_recv.at[block, me],
            peer,
            slab,
        )

    def keep(block):
        return pltpu.make_async_copy(
            cells_ref.at[block, rows(me)], columns(out_ref, block_of(me, block)), out_local.at[block]
        )

    opposite = jnp.where(at < line // 2, 2, 0)
    group = member_n // 4

    @pl.loop(0, slots)
    def _(block):
        @pl.when((block >= 2) & (ahead - 2 + block < slots))
        def _():
            first(ahead - 2 + block)

        picks = choices_of(1, block)
        row = gains(cells_ref[block], picks, tiles_ref, scratch2, gain_ref)

        def part_of(turn):
            q = lax.rem(turn + opposite, 4)
            at_q = rows_of(q)
            part = cells_ref[block, at_q]
            cells_ref[block, at_q] = moved(part, at_q, picks, row, scratch2, gain_ref)
            for k in range(group):
                peer = q * group + k

                @pl.when(peer != me)
                def _():
                    give(block, peer).start()

                @pl.when(peer == me)
                def _():
                    keep(block).start()

        @pl.loop(0, 4)
        def _(turn):
            @pl.when((turn >= 2) | (block < nb - 1))
            def _():
                part_of(turn)

    for hop_by in range(1, member_n):
        give_ints(hop_by).wait_send()
    for member in range(member_n):
        spot, same = member // 2, lane == member % 2
        for way in range(2):
            side(member, way).wait_send()
        for item in range(2):
            @pl.when(same & (spot <= at) & (at < line - 1))
            def _():
                hop(item, member, 0, mate).wait_send()

            @pl.when(same & (spot >= at) & (at > 0))
            def _():
                hop(item, member, 1, mate).wait_send()

            @pl.when(same)
            def _():
                hop(item, member, 2, mate).wait_send()
    for o in range(ob):
        back_near(o).wait_send()
        for q in range(4):
            back_far(o, q).wait_send()

    @pl.loop(0, slots)
    def _(block):
        keep(block).wait()
        for hop_by in range(1, member_n):
            take(block, hop_by).wait_send()
            peer = lax.rem(me + hop_by, member_n)

            @pl.when(reached(peer, block))
            def _():
                give(block, peer).wait_send()
                send(
                    cells_ref.at[block, rows(peer)],
                    columns(out_ref, block_of(peer, block)),
                    out_send.at[block, peer],
                    out_recv.at[block, peer],
                    peer,
                    slab,
                ).wait_recv()


def per_device(
    states, obs_values, obs_weights, obs_cell, op_select, op_table, loc_obs, loc_tile, loc_tiles
):
    member_n, space_n = lax.axis_size("member"), lax.axis_size("space")
    share, width = states.shape
    members = share * member_n
    ob = obs_cell.shape[2]
    batches, _, nb, loc = loc_obs.shape
    codes = jnp.stack([loc_obs, loc_tile]).reshape(2 * batches, nb * loc)
    f32, bf16, i32 = jnp.float32, jnp.bfloat16, jnp.int32
    hbm = pl.BlockSpec(memory_space=pltpu.HBM)
    dma = pltpu.SemaphoreType.DMA
    parts = [
        pltpu.VMEM((3 * ob, members, BLK), bf16),
        pltpu.VMEM((3 * ob, members, BLK), bf16),
        pltpu.VMEM((3 * ob, 1, BLK), f32),
        pltpu.VMEM((3 * ob, 1, BLK), f32),
    ]
    return pl.pallas_call(
        functools.partial(kernel, member_n, space_n, max(2, nb - 3)),
        out_shape=jax.ShapeDtypeStruct((share, width), f32),
        in_specs=[hbm] * 8,
        out_specs=pl.BlockSpec(memory_space=pl.ANY),
        scratch_shapes=[
            pltpu.SMEM(obs_cell.shape, i32),
            pltpu.SMEM(op_select.shape, i32),
            pltpu.VMEM(obs_values.shape, f32),
            pltpu.VMEM(obs_weights.shape, f32),
            pltpu.VMEM(op_table.shape, f32),
            pltpu.VMEM(loc_tiles.shape, f32),
            pltpu.SMEM((member_n,) + codes.shape, i32),
            pltpu.VMEM((member_n,) + codes.shape, i32),
            pltpu.VMEM((width // BLK, share, BLK), f32),
            pltpu.VMEM((nb + 1, members, BLK), f32),
            pltpu.VMEM((ob, members, BLK), f32),
            pltpu.VMEM((3, ob, members, BLK), f32),
            pltpu.VMEM((3, ob, members, BLK), f32),
            pltpu.VMEM((2 * BLK, loc * BLK), bf16),
        ] + parts + parts + [
            dma((width // BLK,)),
            dma((8,)),
            dma((member_n,)),
            dma((member_n,)),
            dma((2, member_n, 3)),
            dma((2, member_n)),
            dma((member_n, 2)),
            dma((member_n, 2)),
            dma((nb + 1, member_n)),
            dma((nb + 1, member_n)),
            dma((nb + 1,)),
            dma((ob,)),
            dma((ob,)),
            dma((ob,)),
            dma((ob,)),
            dma((ob, 4)),
            dma((ob, 4)),
            dma((nb + 1, member_n)),
            dma((nb + 1, member_n)),
            dma((nb + 1,)),
        ],
        compiler_params=pltpu.CompilerParams(
            vmem_limit_bytes=58 * 1024 * 1024, collective_id=0, has_side_effects=True
        ),
    )(obs_cell, op_select, obs_values, obs_weights, op_table, codes, states, loc_tiles)


def solution(mesh):
    placed = (
        P("member", "space"),
        P(),
        P(),
        P(None, "space", None),
        P(None, "space", None),
        P(),
        P(None, "space", "member", None),
        P(None, "space", "member", None),
        P(),
    )
    return jax.shard_map(
        per_device, mesh=mesh, in_specs=placed, out_specs=P("member", "space"), check_vma=False
    )
```

```python
import functools

import jax
import jax.numpy as jnp
from jax import lax
from jax.experimental import pallas as pl
from jax.experimental.pallas import tpu as pltpu
from jax.sharding import PartitionSpec as P

BLK = 128
NT_DIMS = (((1,), (1,)), ((), ()))


def split(x):
    hi = x.astype(jnp.bfloat16)
    lo = (x - hi.astype(jnp.float32)).astype(jnp.bfloat16)
    return hi, lo


def dot(a, b):
    return jnp.dot(a, b, preferred_element_type=jnp.float32)


def dot_nt(a, b):
    return lax.dot_general(a, b, NT_DIMS, preferred_element_type=jnp.float32)


def observe(block, operator):
    hi, lo = split(block)
    op_hi, op_lo = split(operator)
    part = dot_nt(hi, jnp.concatenate([op_hi, op_lo], axis=0))
    return part[:, :BLK] + part[:, BLK:] + dot_nt(lo, op_hi)


def send(src, dst, send_sem, recv_sem, member, space):
    return pltpu.make_async_remote_copy(
        src_ref=src,
        dst_ref=dst,
        send_sem=send_sem,
        recv_sem=recv_sem,
        device_id=(member, space),
        device_id_type=pl.DeviceIdType.MESH,
    )


def columns(ref, block):
    return ref.at[:, pl.ds(pl.multiple_of(block * BLK, BLK), BLK)]


def load_block(batch, place, o, source, window_ref, values_ref, weights_ref, scratch):
    hi_ref, lo_ref, d_ref, w_ref = scratch
    _, ob, members, _ = window_ref.shape
    j = place * ob + o
    at = pl.ds(pl.multiple_of((source * ob + o) * BLK, BLK), BLK)
    weight = weights_ref[batch:batch + 1, at]
    block = window_ref[place, o]
    mean = jnp.sum(block, axis=0, keepdims=True) * (1.0 / members)
    hi, lo = split(block - mean)
    hi_ref[j] = hi
    lo_ref[j] = lo
    w_ref[j] = weight
    d_ref[j] = weight * (values_ref[batch:batch + 1, at] - mean)


def load_window(batch, place, source, window_ref, *rest):
    for o in range(window_ref.shape[1]):
        load_block(batch, place, o, source, window_ref, *rest)


def gains(cell, picks, tiles_ref, scratch, gain_ref):
    hi_ref, lo_ref, d_ref, w_ref = scratch
    members = cell.shape[0]
    mean = jnp.sum(cell, axis=0, keepdims=True) * (1.0 / members)
    hi, lo = split(jnp.transpose(cell - mean))
    both = jnp.concatenate([hi, lo], axis=0)
    ones = []
    for pair in range(len(picks) // 2):
        (first, tile_a), (second, tile_b) = picks[2 * pair], picks[2 * pair + 1]
        obs_hi = jnp.concatenate([hi_ref[first], hi_ref[second]], axis=1)
        obs_lo = jnp.concatenate([lo_ref[first], lo_ref[second]], axis=1)
        part = dot(both, obs_hi)
        cov = part[:BLK] + part[BLK:] + dot(hi, obs_lo)
        tile = jnp.concatenate([tiles_ref[tile_a], tiles_ref[tile_b]], axis=1)
        gain = tile * (cov * (1.0 / (members - 1)))
        d = jnp.concatenate([d_ref[first], d_ref[second]], axis=1)
        w = jnp.concatenate([w_ref[first], w_ref[second]], axis=1)
        ones.append(jnp.sum(gain * d, axis=1, keepdims=True))
        gain_hi, gain_lo = split(gain * (-0.5 * w))
        gain_ref[:BLK, 2 * pair * BLK:2 * (pair + 1) * BLK] = gain_hi
        gain_ref[BLK:, 2 * pair * BLK:2 * (pair + 1) * BLK] = gain_lo
    shift = functools.reduce(jnp.add, ones)
    return jnp.transpose(jnp.broadcast_to(shift, (BLK, BLK)))[:1]


def moved(part, at, picks, row, scratch, gain_ref):
    hi_ref, lo_ref = scratch[:2]
    obs_hi = jnp.concatenate([hi_ref[j, at] for j, _ in picks], axis=1)
    obs_lo = jnp.concatenate([lo_ref[j, at] for j, _ in picks], axis=1)
    step = dot_nt(obs_hi, gain_ref[...])
    return part + (step[:, :BLK] + step[:, BLK:] + dot_nt(obs_lo, gain_ref[:BLK]) + row)


def kernel(member_n, space_n, ahead, *refs):
    sources, states_hbm, tiles_hbm, out_ref, refs = refs[:6], refs[6], refs[7], refs[8], refs[9:]
    copies, (tiles_ref, table_of_ints, ints_ref), refs = refs[:5], refs[5:8], refs[8:]
    cell_ref, op_ref, values_ref, weights_ref, table_ref = copies
    states_ref, cells_ref, picks_ref, win1_ref, win2_ref, gain_ref = refs[:6]
    scratch1, scratch2, refs = refs[6:10], refs[10:14], refs[14:]
    load_sem, local_sem, ints_send, ints_recv, hop_send, hop_recv, halo_send, halo_recv = refs[:8]
    in_send, in_recv, in_local, back_send, back_recv = refs[8:13]
    far_send, far_recv, out_send, out_recv, out_local = refs[13:]
    codes_hbm = sources[5]

    slots, members, _ = cells_ref.shape
    nb = slots - 1
    ob = picks_ref.shape[0]
    share = states_ref.shape[1]
    batches = cell_ref.shape[0]
    loc = codes_hbm.shape[1] // nb
    me = lax.axis_index("member")
    slab = lax.axis_index("space")
    after = lax.rem(slab + 1, space_n)
    before = lax.rem(slab + space_n - 1, space_n)
    line = member_n // 2
    at, lane = me // 2, lax.rem(me, 2)
    mate = at * 2 + 1 - lane
    odd = lax.rem(slab, 2)
    near, far = 2 * (1 - odd), 2 * odd
    near_slab = slab + 1 - 2 * odd
    far_slab = lax.rem(slab + space_n - 1 + 2 * odd, space_n)
    quarter = members // 4
    half = member_n // 2
    partner = lax.rem(me + half, member_n)

    def block_of(member, slot):
        other = lax.rem(member + half, member_n)
        return jnp.where(slot < nb, member * nb + slot, other * nb + nb - 1)

    def reached(member, slot):
        return (slot < nb - 1) | (member // half == me // half)

    barrier = pltpu.get_barrier_semaphore()

    def greet(member, space):
        pl.semaphore_signal(
            barrier, inc=1, device_id=(member, space), device_id_type=pl.DeviceIdType.MESH
        )

    greet(me, after)
    greet(me, before)
    for hop_by in range(1, member_n):
        greet(lax.rem(me + hop_by, member_n), slab)

    small = [
        pltpu.make_async_copy(sources[i], copies[i], local_sem.at[i]) for i in range(len(copies))
    ]
    for copy in small:
        copy.start()

    def load(block):
        return pltpu.make_async_copy(
            columns(states_hbm, block), states_ref.at[block], load_sem.at[block]
        )

    @pl.loop(0, member_n * nb)
    def _(block):
        load(block).start()

    tiles_copy = pltpu.make_async_copy(tiles_hbm, tiles_ref, local_sem.at[5])
    tiles_copy.start()
    keep_ints = pltpu.make_async_copy(codes_hbm, ints_ref.at[me], local_sem.at[6])
    keep_ints.start()

    def rows(member):
        return pl.ds(pl.multiple_of(member * share, 8), share)

    for copy in small:
        copy.wait()

    @pl.loop(0, member_n * nb)
    def _(block):
        load(block).wait()

    own_ref = win1_ref.at[1]
    for o in range(ob):
        own_ref[o, rows(me)] = observe(states_ref[cell_ref[0, 0, o]], table_ref[op_ref[0, 0, o]])
    for o in range(ob):
        picks_ref[o, rows(me)] = states_ref[cell_ref[1, 0, o]]
    pl.semaphore_wait(barrier, member_n + 1)

    def hop(item, member, way, target):
        part = (own_ref, picks_ref)[item].at[:, rows(member)]
        return send(
            part, part, hop_send.at[item, member, way], hop_recv.at[item, member], target, slab
        )

    def side(member, way):
        return send(
            own_ref.at[:, rows(member)],
            win1_ref.at[2 * way, :, rows(member)],
            halo_send.at[member, way],
            halo_recv.at[member, way],
            me,
            (after, before)[way],
        )

    def pass_on(item, member, up, down, across):
        if up:
            @pl.when(at < line - 1)
            def _():
                hop(item, member, 0, me + 2).start()

        if down:
            @pl.when(at > 0)
            def _():
                hop(item, member, 1, me - 2).start()

        if across:
            hop(item, member, 2, mate).start()
        if item == 0:
            side(member, 0).start()
            side(member, 1).start()

    def landed(item, member):
        hop(item, member, 2, mate).wait_recv()

    def take(block, hop_by):
        peer = lax.rem(me + hop_by, member_n)
        return send(
            states_ref.at[block_of(peer, block)],
            cells_ref.at[block, rows(me)],
            in_send.at[block, hop_by],
            in_recv.at[block, me],
            peer,
            slab,
        )

    def stay(block):
        return pltpu.make_async_copy(
            states_ref.at[block_of(me, block)], cells_ref.at[block, rows(me)], in_local.at[block]
        )

    hops = sorted(range(1, member_n), key=lambda k: (abs(k - line), k))

    def straight(block):
        for hop_by in hops:
            if hop_by % 2 == 0:
                take(block, hop_by).start()
        stay(block).start()

    def crossing(block):
        for hop_by in hops:
            if hop_by % 2 == 1:
                take(block, hop_by).start()

    waiting = list(range(slots))

    def feed(count=1):
        for _ in range(min(count, len(waiting))):
            straight(waiting.pop(0))

    def give_ints(hop_by):
        peer = lax.rem(me + hop_by, member_n)
        return send(
            codes_hbm, ints_ref.at[me], ints_send.at[hop_by], ints_recv.at[me], peer, slab
        )

    pass_on(0, me, True, True, True)
    for hop_by in range(1, member_n):
        give_ints(hop_by).start()
    pass_on(1, me, True, True, True)
    feed()

    for item in range(2):
        for step in range(1, line):
            low, high = me - 2 * step, me + 2 * step

            @pl.when(low >= 0)
            def _():
                landed(item, low)
                pass_on(item, low, True, False, True)

            @pl.when(high < member_n)
            def _():
                landed(item, high)
                pass_on(item, high, False, True, True)

            if step == 1:
                feed()
            gap = 2 * (step - 1)
            if gap == 0:
                landed(item, mate)
                pass_on(item, mate, False, False, False)
            else:
                @pl.when(mate - gap >= 0)
                def _():
                    landed(item, mate - gap)
                    pass_on(item, mate - gap, False, False, False)

                @pl.when(mate + gap < member_n)
                def _():
                    landed(item, mate + gap)
                    pass_on(item, mate + gap, False, False, False)

        gap = 2 * (line - 1)

        @pl.when(mate - gap >= 0)
        def _():
            landed(item, mate - gap)
            pass_on(item, mate - gap, False, False, False)

        @pl.when(mate + gap < member_n)
        def _():
            landed(item, mate + gap)
            pass_on(item, mate + gap, False, False, False)

        if item == 0:
            feed()

    feed(slots)

    @pl.loop(0, slots)
    def _(block):
        crossing(block)

    keep_ints.wait()
    for hop_by in range(1, member_n):
        peer = lax.rem(me + hop_by, member_n)
        send(
            codes_hbm, ints_ref.at[peer], ints_send.at[hop_by], ints_recv.at[peer], peer, slab
        ).wait_recv()
    scalars = pltpu.make_async_copy(ints_ref, table_of_ints, local_sem.at[7])
    scalars.start()

    def source_of(place):
        return lax.rem(slab + space_n - 1 + place, space_n)

    load_window(0, 1, slab, win1_ref, values_ref, weights_ref, scratch1)
    for way in range(2):
        for member in range(member_n):
            side(member, way).wait_recv()
    for place in (near, far):
        load_window(0, place, source_of(place), win1_ref, values_ref, weights_ref, scratch1)
    scalars.wait()
    tiles_copy.wait()

    def choices_of(batch, slot):
        owner = jnp.where(slot < nb, me, partner)
        return choices(batch, owner, jnp.where(slot < nb, slot, nb - 1))

    def choices(batch, owner, block):
        return [
            (
                table_of_ints[owner, batch, block * loc + l],
                table_of_ints[owner, batches + batch, block * loc + l],
            )
            for l in range(loc)
        ]

    def back_near(o):
        return send(
            win2_ref.at[1, o],
            win2_ref.at[far, o],
            back_send.at[o],
            back_recv.at[o],
            me,
            near_slab,
        )

    def rows_of(q):
        return pl.ds(pl.multiple_of(q * quarter, 16), quarter)

    def back_far(o, q):
        return send(
            win2_ref.at[1, o, rows_of(q)],
            win2_ref.at[near, o, rows_of(q)],
            far_send.at[o, q],
            far_recv.at[o, q],
            me,
            far_slab,
        )

    @pl.loop(0, ob)
    def _(o):
        cell = cell_ref[1, 0, o]
        owner = cell // nb
        picks = choices(0, owner, cell - owner * nb)
        row = gains(picks_ref[o], picks, tiles_ref, scratch1, gain_ref)
        operator = table_ref[op_ref[1, 0, o]]

        @pl.loop(0, 4)
        def _(turn):
            q = turn
            at_q = rows_of(q)
            fresh = moved(picks_ref[o, at_q], at_q, picks, row, scratch1, gain_ref)
            win2_ref[1, o, at_q] = observe(fresh, operator)

            back_far(o, q).start()

        back_near(o).start()


    load_window(1, 1, slab, win2_ref, values_ref, weights_ref, scratch2)

    def first(block):
        stay(block).wait()
        for hop_by in range(1, member_n):
            peer = lax.rem(me + hop_by, member_n)
            send(
                states_ref.at[block_of(peer, block)],
                cells_ref.at[block, rows(peer)],
                in_send.at[block, hop_by],
                in_recv.at[block, peer],
                peer,
                slab,
            ).wait_recv()
        picks = choices_of(0, block)
        row = gains(cells_ref[block], picks, tiles_ref, scratch1, gain_ref)

        @pl.loop(0, 4)
        def _(q):
            at_q = rows_of(q)
            part = cells_ref[block, at_q]
            cells_ref[block, at_q] = moved(part, at_q, picks, row, scratch1, gain_ref)

    @pl.loop(0, ahead)
    def _(block):
        first(block)


    for o in range(ob):
        back_near(o).wait_recv()
    load_window(1, near, source_of(near), win2_ref, values_ref, weights_ref, scratch2)
    for o in range(ob):
        for q in range(4):
            back_far(o, q).wait_recv()
        load_block(1, far, o, source_of(far), win2_ref, values_ref, weights_ref, scratch2)

    def give(block, peer):
        return send(
            cells_ref.at[block, rows(peer)],
            columns(out_ref, block_of(me, block)),
            out_send.at[block, peer],
            out_recv.at[block, me],
            peer,
            slab,
        )

    def keep(block):
        return pltpu.make_async_copy(
            cells_ref.at[block, rows(me)], columns(out_ref, block_of(me, block)), out_local.at[block]
        )

    opposite = jnp.where(at < line // 2, 2, 0)
    group = member_n // 4

    @pl.loop(0, slots)
    def _(block):
        @pl.when((block >= 2) & (ahead - 2 + block < slots))
        def _():
            first(ahead - 2 + block)

        picks = choices_of(1, block)
        row = gains(cells_ref[block], picks, tiles_ref, scratch2, gain_ref)

        def part_of(turn):
            q = lax.rem(turn + opposite, 4)
            at_q = rows_of(q)
            part = cells_ref[block, at_q]
            cells_ref[block, at_q] = moved(part, at_q, picks, row, scratch2, gain_ref)
            for k in range(group):
                peer = q * group + k

                @pl.when(peer != me)
                def _():
                    give(block, peer).start()

                @pl.when(peer == me)
                def _():
                    keep(block).start()

        @pl.loop(0, 4)
        def _(turn):
            @pl.when((turn >= 2) | (block < nb - 1))
            def _():
                part_of(turn)

    for hop_by in range(1, member_n):
        give_ints(hop_by).wait_send()
    for member in range(member_n):
        spot, same = member // 2, lane == member % 2
        for way in range(2):
            side(member, way).wait_send()
        for item in range(2):
            @pl.when(same & (spot <= at) & (at < line - 1))
            def _():
                hop(item, member, 0, mate).wait_send()

            @pl.when(same & (spot >= at) & (at > 0))
            def _():
                hop(item, member, 1, mate).wait_send()

            @pl.when(same)
            def _():
                hop(item, member, 2, mate).wait_send()
    for o in range(ob):
        back_near(o).wait_send()
        for q in range(4):
            back_far(o, q).wait_send()

    @pl.loop(0, slots)
    def _(block):
        keep(block).wait()
        for hop_by in range(1, member_n):
            take(block, hop_by).wait_send()
            peer = lax.rem(me + hop_by, member_n)

            @pl.when(reached(peer, block))
            def _():
                give(block, peer).wait_send()
                send(
                    cells_ref.at[block, rows(peer)],
                    columns(out_ref, block_of(peer, block)),
                    out_send.at[block, peer],
                    out_recv.at[block, peer],
                    peer,
                    slab,
                ).wait_recv()


def copy_kernel(source_ref, out_ref, buffer_ref, load_sem, store_sem):
    steps, tall = load_sem.shape[0], source_ref.shape[0] // load_sem.shape[0]

    def load(i):
        at = pl.ds(i * tall, tall)
        return pltpu.make_async_copy(source_ref.at[at], buffer_ref.at[at], load_sem.at[i])

    def store(i):
        at = pl.ds(i * tall, tall)
        return pltpu.make_async_copy(buffer_ref.at[at], out_ref.at[at], store_sem.at[i])

    for i in range(steps):
        load(i).start()
    for i in range(steps):
        load(i).wait()
        store(i).start()
    for i in range(steps):
        store(i).wait()


def copied(array):
    steps = max(1, array.shape[0] // 8)
    return pl.pallas_call(
        copy_kernel,
        out_shape=jax.ShapeDtypeStruct(array.shape, array.dtype),
        in_specs=[pl.BlockSpec(memory_space=pl.ANY)],
        out_specs=pl.BlockSpec(memory_space=pl.ANY),
        scratch_shapes=[
            pltpu.VMEM(array.shape, array.dtype),
            pltpu.SemaphoreType.DMA((steps,)),
            pltpu.SemaphoreType.DMA((steps,)),
        ],
        compiler_params=pltpu.CompilerParams(vmem_limit_bytes=58 * 1024 * 1024),
    )(array)


def per_device(
    states, obs_values, obs_weights, obs_cell, op_select, op_table, loc_obs, loc_tile, loc_tiles
):
    member_n, space_n = lax.axis_size("member"), lax.axis_size("space")
    share, width = states.shape
    members = share * member_n
    ob = obs_cell.shape[2]
    batches, _, nb, loc = loc_obs.shape
    codes = jnp.stack([loc_obs, loc_tile]).reshape(2 * batches, nb * loc)
    f32, bf16, i32 = jnp.float32, jnp.bfloat16, jnp.int32
    hbm = pl.BlockSpec(memory_space=pltpu.HBM)
    dma = pltpu.SemaphoreType.DMA
    parts = [
        pltpu.VMEM((3 * ob, members, BLK), bf16),
        pltpu.VMEM((3 * ob, members, BLK), bf16),
        pltpu.VMEM((3 * ob, 1, BLK), f32),
        pltpu.VMEM((3 * ob, 1, BLK), f32),
    ]
    result = pl.pallas_call(
        functools.partial(kernel, member_n, space_n, 2),
        out_shape=jax.ShapeDtypeStruct((share, width), f32),
        in_specs=[hbm] * 8,
        out_specs=pl.BlockSpec(memory_space=pl.ANY),
        scratch_shapes=[
            pltpu.SMEM(obs_cell.shape, i32),
            pltpu.SMEM(op_select.shape, i32),
            pltpu.VMEM(obs_values.shape, f32),
            pltpu.VMEM(obs_weights.shape, f32),
            pltpu.VMEM(op_table.shape, f32),
            pltpu.VMEM(loc_tiles.shape, f32),
            pltpu.SMEM((member_n,) + codes.shape, i32),
            pltpu.VMEM((member_n,) + codes.shape, i32),
            pltpu.VMEM((width // BLK, share, BLK), f32),
            pltpu.VMEM((nb + 1, members, BLK), f32),
            pltpu.VMEM((ob, members, BLK), f32),
            pltpu.VMEM((3, ob, members, BLK), f32),
            pltpu.VMEM((3, ob, members, BLK), f32),
            pltpu.VMEM((2 * BLK, loc * BLK), bf16),
        ] + parts + parts + [
            dma((width // BLK,)),
            dma((8,)),
            dma((member_n,)),
            dma((member_n,)),
            dma((2, member_n, 3)),
            dma((2, member_n)),
            dma((member_n, 2)),
            dma((member_n, 2)),
            dma((nb + 1, member_n)),
            dma((nb + 1, member_n)),
            dma((nb + 1,)),
            dma((ob,)),
            dma((ob,)),
            dma((ob, 4)),
            dma((ob, 4)),
            dma((nb + 1, member_n)),
            dma((nb + 1, member_n)),
            dma((nb + 1,)),
        ],
        compiler_params=pltpu.CompilerParams(
            vmem_limit_bytes=58 * 1024 * 1024, collective_id=0, has_side_effects=True
        ),
    )(obs_cell, op_select, obs_values, obs_weights, op_table, codes, states, loc_tiles)
    return copied(result)


def solution(mesh):
    placed = (
        P("member", "space"),
        P(),
        P(),
        P(None, "space", None),
        P(None, "space", None),
        P(),
        P(None, "space", "member", None),
        P(None, "space", "member", None),
        P(),
    )
    return jax.shard_map(
        per_device, mesh=mesh, in_specs=placed, out_specs=P("member", "space"), check_vma=False
    )
```

```python
import functools

import jax
import jax.numpy as jnp
from jax import lax
from jax.experimental import pallas as pl
from jax.experimental.pallas import tpu as pltpu
from jax.sharding import PartitionSpec as P

BLK = 128
NT_DIMS = (((1,), (1,)), ((), ()))


def split(x):
    hi = x.astype(jnp.bfloat16)
    lo = (x - hi.astype(jnp.float32)).astype(jnp.bfloat16)
    return hi, lo


def dot(a, b):
    return jnp.dot(a, b, preferred_element_type=jnp.float32)


def dot_nt(a, b):
    return lax.dot_general(a, b, NT_DIMS, preferred_element_type=jnp.float32)


def observe(block, operator):
    hi, lo = split(block)
    op_hi, op_lo = split(operator)
    part = dot_nt(hi, jnp.concatenate([op_hi, op_lo], axis=0))
    return part[:, :BLK] + part[:, BLK:] + dot_nt(lo, op_hi)


def send(src, dst, send_sem, recv_sem, member, space):
    return pltpu.make_async_remote_copy(
        src_ref=src,
        dst_ref=dst,
        send_sem=send_sem,
        recv_sem=recv_sem,
        device_id=(member, space),
        device_id_type=pl.DeviceIdType.MESH,
    )


def columns(ref, block):
    return ref.at[:, pl.ds(pl.multiple_of(block * BLK, BLK), BLK)]


def load_block(batch, place, o, source, window_ref, values_ref, weights_ref, scratch):
    hi_ref, lo_ref, d_ref, w_ref = scratch
    _, ob, members, _ = window_ref.shape
    j = place * ob + o
    at = pl.ds(pl.multiple_of((source * ob + o) * BLK, BLK), BLK)
    weight = weights_ref[batch:batch + 1, at]
    block = window_ref[place, o]
    mean = jnp.sum(block, axis=0, keepdims=True) * (1.0 / members)
    hi, lo = split(block - mean)
    hi_ref[j] = hi
    lo_ref[j] = lo
    w_ref[j] = weight
    d_ref[j] = weight * (values_ref[batch:batch + 1, at] - mean)


def load_window(batch, place, source, window_ref, *rest):
    for o in range(window_ref.shape[1]):
        load_block(batch, place, o, source, window_ref, *rest)


def gains(cell, picks, tiles_ref, scratch, gain_ref):
    hi_ref, lo_ref, d_ref, w_ref = scratch
    members = cell.shape[0]
    mean = jnp.sum(cell, axis=0, keepdims=True) * (1.0 / members)
    hi, lo = split(jnp.transpose(cell - mean))
    both = jnp.concatenate([hi, lo], axis=0)
    ones = []
    for pair in range(len(picks) // 2):
        (first, tile_a), (second, tile_b) = picks[2 * pair], picks[2 * pair + 1]
        obs_hi = jnp.concatenate([hi_ref[first], hi_ref[second]], axis=1)
        obs_lo = jnp.concatenate([lo_ref[first], lo_ref[second]], axis=1)
        part = dot(both, obs_hi)
        cov = part[:BLK] + part[BLK:] + dot(hi, obs_lo)
        tile = jnp.concatenate([tiles_ref[tile_a], tiles_ref[tile_b]], axis=1)
        gain = tile * (cov * (1.0 / (members - 1)))
        d = jnp.concatenate([d_ref[first], d_ref[second]], axis=1)
        w = jnp.concatenate([w_ref[first], w_ref[second]], axis=1)
        ones.append(jnp.sum(gain * d, axis=1, keepdims=True))
        gain_hi, gain_lo = split(gain * (-0.5 * w))
        gain_ref[:BLK, 2 * pair * BLK:2 * (pair + 1) * BLK] = gain_hi
        gain_ref[BLK:, 2 * pair * BLK:2 * (pair + 1) * BLK] = gain_lo
    shift = functools.reduce(jnp.add, ones)
    return jnp.transpose(jnp.broadcast_to(shift, (BLK, BLK)))[:1]


def moved(part, at, picks, row, scratch, gain_ref):
    hi_ref, lo_ref = scratch[:2]
    obs_hi = jnp.concatenate([hi_ref[j, at] for j, _ in picks], axis=1)
    obs_lo = jnp.concatenate([lo_ref[j, at] for j, _ in picks], axis=1)
    step = dot_nt(obs_hi, gain_ref[...])
    return part + (step[:, :BLK] + step[:, BLK:] + dot_nt(obs_lo, gain_ref[:BLK]) + row)


def kernel(member_n, space_n, ahead, *refs):
    sources, states_hbm, tiles_hbm, out_ref, refs = refs[:6], refs[6], refs[7], refs[8], refs[9:]
    copies, (tiles_ref, table_of_ints, ints_ref), refs = refs[:5], refs[5:8], refs[8:]
    cell_ref, op_ref, values_ref, weights_ref, table_ref = copies
    states_ref, cells_ref, picks_ref, win1_ref, win2_ref, gain_ref = refs[:6]
    scratch1, scratch2, refs = refs[6:10], refs[10:14], refs[14:]
    load_sem, local_sem, ints_send, ints_recv, hop_send, hop_recv, halo_send, halo_recv = refs[:8]
    in_send, in_recv, in_local, back_send, back_recv = refs[8:13]
    far_send, far_recv, out_send, out_recv, out_local = refs[13:]
    codes_hbm = sources[5]

    slots, members, _ = cells_ref.shape
    nb = slots - 1
    ob = picks_ref.shape[0]
    share = states_ref.shape[1]
    batches = cell_ref.shape[0]
    loc = codes_hbm.shape[1] // nb
    me = lax.axis_index("member")
    slab = lax.axis_index("space")
    after = lax.rem(slab + 1, space_n)
    before = lax.rem(slab + space_n - 1, space_n)
    line = member_n // 2
    at, lane = me // 2, lax.rem(me, 2)
    mate = at * 2 + 1 - lane
    odd = lax.rem(slab, 2)
    near, far = 2 * (1 - odd), 2 * odd
    near_slab = slab + 1 - 2 * odd
    far_slab = lax.rem(slab + space_n - 1 + 2 * odd, space_n)
    quarter = members // 4
    half = member_n // 2
    partner = lax.rem(me + half, member_n)

    def block_of(member, slot):
        other = lax.rem(member + half, member_n)
        return jnp.where(slot < nb, member * nb + slot, other * nb + nb - 1)

    def reached(member, slot):
        return (slot < nb - 1) | (member // half == me // half)

    barrier = pltpu.get_barrier_semaphore()

    def greet(member, space):
        pl.semaphore_signal(
            barrier, inc=1, device_id=(member, space), device_id_type=pl.DeviceIdType.MESH
        )

    greet(me, after)
    greet(me, before)
    for hop_by in range(1, member_n):
        greet(lax.rem(me + hop_by, member_n), slab)

    small = [
        pltpu.make_async_copy(sources[i], copies[i], local_sem.at[i]) for i in range(len(copies))
    ]
    for copy in small:
        copy.start()

    def load(block):
        return pltpu.make_async_copy(
            columns(states_hbm, block), states_ref.at[block], load_sem.at[block]
        )

    @pl.loop(0, member_n * nb)
    def _(block):
        load(block).start()

    tiles_copy = pltpu.make_async_copy(tiles_hbm, tiles_ref, local_sem.at[5])
    tiles_copy.start()
    keep_ints = pltpu.make_async_copy(codes_hbm, ints_ref.at[me], local_sem.at[6])
    keep_ints.start()

    def rows(member):
        return pl.ds(pl.multiple_of(member * share, 8), share)

    for copy in small:
        copy.wait()

    @pl.loop(0, member_n * nb)
    def _(block):
        load(block).wait()

    own_ref = win1_ref.at[1]
    for o in range(ob):
        own_ref[o, rows(me)] = observe(states_ref[cell_ref[0, 0, o]], table_ref[op_ref[0, 0, o]])
    for o in range(ob):
        picks_ref[o, rows(me)] = states_ref[cell_ref[1, 0, o]]
    pl.semaphore_wait(barrier, member_n + 1)

    def hop(item, member, way, target):
        part = (own_ref, picks_ref)[item].at[:, rows(member)]
        return send(
            part, part, hop_send.at[item, member, way], hop_recv.at[item, member], target, slab
        )

    def side(member, way):
        return send(
            own_ref.at[:, rows(member)],
            win1_ref.at[2 * way, :, rows(member)],
            halo_send.at[member, way],
            halo_recv.at[member, way],
            me,
            (after, before)[way],
        )

    def pass_on(item, member, up, down, across):
        if up:
            @pl.when(at < line - 1)
            def _():
                hop(item, member, 0, me + 2).start()

        if down:
            @pl.when(at > 0)
            def _():
                hop(item, member, 1, me - 2).start()

        if across:
            hop(item, member, 2, mate).start()
        if item == 0:
            side(member, 0).start()
            side(member, 1).start()

    def landed(item, member):
        hop(item, member, 2, mate).wait_recv()

    def take(block, hop_by):
        peer = lax.rem(me + hop_by, member_n)
        return send(
            states_ref.at[block_of(peer, block)],
            cells_ref.at[block, rows(me)],
            in_send.at[block, hop_by],
            in_recv.at[block, me],
            peer,
            slab,
        )

    def stay(block):
        return pltpu.make_async_copy(
            states_ref.at[block_of(me, block)], cells_ref.at[block, rows(me)], in_local.at[block]
        )

    hops = sorted(range(1, member_n), key=lambda k: (abs(k - line), k))

    def straight(block):
        for hop_by in hops:
            if hop_by % 2 == 0:
                take(block, hop_by).start()
        stay(block).start()

    def crossing(block):
        for hop_by in hops:
            if hop_by % 2 == 1:
                take(block, hop_by).start()

    waiting = list(range(slots))

    def feed(count=1):
        for _ in range(min(count, len(waiting))):
            straight(waiting.pop(0))

    def give_ints(hop_by):
        peer = lax.rem(me + hop_by, member_n)
        return send(
            codes_hbm, ints_ref.at[me], ints_send.at[hop_by], ints_recv.at[me], peer, slab
        )

    pass_on(0, me, True, True, True)
    for hop_by in range(1, member_n):
        give_ints(hop_by).start()
    pass_on(1, me, True, True, True)
    feed()

    for item in range(2):
        for step in range(1, line):
            low, high = me - 2 * step, me + 2 * step

            @pl.when(low >= 0)
            def _():
                landed(item, low)
                pass_on(item, low, True, False, True)

            @pl.when(high < member_n)
            def _():
                landed(item, high)
                pass_on(item, high, False, True, True)

            if item == 1:
                feed()
            gap = 2 * (step - 1)
            if gap == 0:
                landed(item, mate)
                pass_on(item, mate, False, False, False)
            else:
                @pl.when(mate - gap >= 0)
                def _():
                    landed(item, mate - gap)
                    pass_on(item, mate - gap, False, False, False)

                @pl.when(mate + gap < member_n)
                def _():
                    landed(item, mate + gap)
                    pass_on(item, mate + gap, False, False, False)

        gap = 2 * (line - 1)

        @pl.when(mate - gap >= 0)
        def _():
            landed(item, mate - gap)
            pass_on(item, mate - gap, False, False, False)

        @pl.when(mate + gap < member_n)
        def _():
            landed(item, mate + gap)
            pass_on(item, mate + gap, False, False, False)

        if item == 0:
            feed()

    feed(slots)

    @pl.loop(0, slots)
    def _(block):
        crossing(block)

    keep_ints.wait()
    for hop_by in range(1, member_n):
        peer = lax.rem(me + hop_by, member_n)
        send(
            codes_hbm, ints_ref.at[peer], ints_send.at[hop_by], ints_recv.at[peer], peer, slab
        ).wait_recv()
    scalars = pltpu.make_async_copy(ints_ref, table_of_ints, local_sem.at[7])
    scalars.start()

    def source_of(place):
        return lax.rem(slab + space_n - 1 + place, space_n)

    load_window(0, 1, slab, win1_ref, values_ref, weights_ref, scratch1)
    for way in range(2):
        for member in range(member_n):
            side(member, way).wait_recv()
    for place in (near, far):
        load_window(0, place, source_of(place), win1_ref, values_ref, weights_ref, scratch1)
    scalars.wait()
    tiles_copy.wait()

    def choices_of(batch, slot):
        owner = jnp.where(slot < nb, me, partner)
        return choices(batch, owner, jnp.where(slot < nb, slot, nb - 1))

    def choices(batch, owner, block):
        return [
            (
                table_of_ints[owner, batch, block * loc + l],
                table_of_ints[owner, batches + batch, block * loc + l],
            )
            for l in range(loc)
        ]

    def back_near(o):
        return send(
            win2_ref.at[1, o],
            win2_ref.at[far, o],
            back_send.at[o],
            back_recv.at[o],
            me,
            near_slab,
        )

    def rows_of(q):
        return pl.ds(pl.multiple_of(q * quarter, 16), quarter)

    def back_far(o, q):
        return send(
            win2_ref.at[1, o, rows_of(q)],
            win2_ref.at[near, o, rows_of(q)],
            far_send.at[o, q],
            far_recv.at[o, q],
            me,
            far_slab,
        )

    @pl.loop(0, ob)
    def _(o):
        cell = cell_ref[1, 0, o]
        owner = cell // nb
        picks = choices(0, owner, cell - owner * nb)
        row = gains(picks_ref[o], picks, tiles_ref, scratch1, gain_ref)
        operator = table_ref[op_ref[1, 0, o]]

        @pl.loop(0, 4)
        def _(turn):
            q = turn
            at_q = rows_of(q)
            fresh = moved(picks_ref[o, at_q], at_q, picks, row, scratch1, gain_ref)
            win2_ref[1, o, at_q] = observe(fresh, operator)

            back_far(o, q).start()

        back_near(o).start()


    load_window(1, 1, slab, win2_ref, values_ref, weights_ref, scratch2)

    def first(block):
        stay(block).wait()
        for hop_by in range(1, member_n):
            peer = lax.rem(me + hop_by, member_n)
            send(
                states_ref.at[block_of(peer, block)],
                cells_ref.at[block, rows(peer)],
                in_send.at[block, hop_by],
                in_recv.at[block, peer],
                peer,
                slab,
            ).wait_recv()
        picks = choices_of(0, block)
        row = gains(cells_ref[block], picks, tiles_ref, scratch1, gain_ref)

        @pl.loop(0, 4)
        def _(q):
            at_q = rows_of(q)
            part = cells_ref[block, at_q]
            cells_ref[block, at_q] = moved(part, at_q, picks, row, scratch1, gain_ref)

    @pl.loop(0, ahead)
    def _(block):
        first(block)


    for o in range(ob):
        back_near(o).wait_recv()
    load_window(1, near, source_of(near), win2_ref, values_ref, weights_ref, scratch2)
    for o in range(ob):
        for q in range(4):
            back_far(o, q).wait_recv()
        load_block(1, far, o, source_of(far), win2_ref, values_ref, weights_ref, scratch2)

    def give(block, peer):
        return send(
            cells_ref.at[block, rows(peer)],
            columns(out_ref, block_of(me, block)),
            out_send.at[block, peer],
            out_recv.at[block, me],
            peer,
            slab,
        )

    def keep(block):
        return pltpu.make_async_copy(
            cells_ref.at[block, rows(me)], columns(out_ref, block_of(me, block)), out_local.at[block]
        )

    opposite = jnp.where(at < line // 2, 2, 0)
    group = member_n // 4

    @pl.loop(0, slots)
    def _(block):
        @pl.when((block >= 2) & (ahead - 2 + block < slots))
        def _():
            first(ahead - 2 + block)

        picks = choices_of(1, block)
        row = gains(cells_ref[block], picks, tiles_ref, scratch2, gain_ref)

        def part_of(turn):
            q = lax.rem(turn + opposite, 4)
            at_q = rows_of(q)
            part = cells_ref[block, at_q]
            cells_ref[block, at_q] = moved(part, at_q, picks, row, scratch2, gain_ref)
            for k in range(group):
                peer = q * group + k

                @pl.when(peer != me)
                def _():
                    give(block, peer).start()

                @pl.when(peer == me)
                def _():
                    keep(block).start()

        @pl.loop(0, 4)
        def _(turn):
            @pl.when((turn >= 2) | (block < nb - 1))
            def _():
                part_of(turn)

    for hop_by in range(1, member_n):
        give_ints(hop_by).wait_send()
    for member in range(member_n):
        spot, same = member // 2, lane == member % 2
        for way in range(2):
            side(member, way).wait_send()
        for item in range(2):
            @pl.when(same & (spot <= at) & (at < line - 1))
            def _():
                hop(item, member, 0, mate).wait_send()

            @pl.when(same & (spot >= at) & (at > 0))
            def _():
                hop(item, member, 1, mate).wait_send()

            @pl.when(same)
            def _():
                hop(item, member, 2, mate).wait_send()
    for o in range(ob):
        back_near(o).wait_send()
        for q in range(4):
            back_far(o, q).wait_send()

    @pl.loop(0, slots)
    def _(block):
        keep(block).wait()
        for hop_by in range(1, member_n):
            take(block, hop_by).wait_send()
            peer = lax.rem(me + hop_by, member_n)

            @pl.when(reached(peer, block))
            def _():
                give(block, peer).wait_send()
                send(
                    cells_ref.at[block, rows(peer)],
                    columns(out_ref, block_of(peer, block)),
                    out_send.at[block, peer],
                    out_recv.at[block, peer],
                    peer,
                    slab,
                ).wait_recv()


def copy_kernel(source_ref, out_ref, buffer_ref, load_sem, store_sem):
    steps, tall = load_sem.shape[0], source_ref.shape[0] // load_sem.shape[0]

    def load(i):
        at = pl.ds(i * tall, tall)
        return pltpu.make_async_copy(source_ref.at[at], buffer_ref.at[at], load_sem.at[i])

    def store(i):
        at = pl.ds(i * tall, tall)
        return pltpu.make_async_copy(buffer_ref.at[at], out_ref.at[at], store_sem.at[i])

    for i in range(steps):
        load(i).start()
    for i in range(steps):
        load(i).wait()
        store(i).start()
    for i in range(steps):
        store(i).wait()


def copied(array):
    steps = max(1, array.shape[0] // 8)
    return pl.pallas_call(
        copy_kernel,
        out_shape=jax.ShapeDtypeStruct(array.shape, array.dtype),
        in_specs=[pl.BlockSpec(memory_space=pl.ANY)],
        out_specs=pl.BlockSpec(memory_space=pl.ANY),
        scratch_shapes=[
            pltpu.VMEM(array.shape, array.dtype),
            pltpu.SemaphoreType.DMA((steps,)),
            pltpu.SemaphoreType.DMA((steps,)),
        ],
        compiler_params=pltpu.CompilerParams(vmem_limit_bytes=58 * 1024 * 1024),
    )(array)


def per_device(
    states, obs_values, obs_weights, obs_cell, op_select, op_table, loc_obs, loc_tile, loc_tiles
):
    member_n, space_n = lax.axis_size("member"), lax.axis_size("space")
    share, width = states.shape
    members = share * member_n
    ob = obs_cell.shape[2]
    batches, _, nb, loc = loc_obs.shape
    codes = jnp.stack([loc_obs, loc_tile]).reshape(2 * batches, nb * loc)
    f32, bf16, i32 = jnp.float32, jnp.bfloat16, jnp.int32
    hbm = pl.BlockSpec(memory_space=pltpu.HBM)
    dma = pltpu.SemaphoreType.DMA
    parts = [
        pltpu.VMEM((3 * ob, members, BLK), bf16),
        pltpu.VMEM((3 * ob, members, BLK), bf16),
        pltpu.VMEM((3 * ob, 1, BLK), f32),
        pltpu.VMEM((3 * ob, 1, BLK), f32),
    ]
    result = pl.pallas_call(
        functools.partial(kernel, member_n, space_n, 2),
        out_shape=jax.ShapeDtypeStruct((share, width), f32),
        in_specs=[hbm] * 8,
        out_specs=pl.BlockSpec(memory_space=pl.ANY),
        scratch_shapes=[
            pltpu.SMEM(obs_cell.shape, i32),
            pltpu.SMEM(op_select.shape, i32),
            pltpu.VMEM(obs_values.shape, f32),
            pltpu.VMEM(obs_weights.shape, f32),
            pltpu.VMEM(op_table.shape, f32),
            pltpu.VMEM(loc_tiles.shape, f32),
            pltpu.SMEM((member_n,) + codes.shape, i32),
            pltpu.VMEM((member_n,) + codes.shape, i32),
            pltpu.VMEM((width // BLK, share, BLK), f32),
            pltpu.VMEM((nb + 1, members, BLK), f32),
            pltpu.VMEM((ob, members, BLK), f32),
            pltpu.VMEM((3, ob, members, BLK), f32),
            pltpu.VMEM((3, ob, members, BLK), f32),
            pltpu.VMEM((2 * BLK, loc * BLK), bf16),
        ] + parts + parts + [
            dma((width // BLK,)),
            dma((8,)),
            dma((member_n,)),
            dma((member_n,)),
            dma((2, member_n, 3)),
            dma((2, member_n)),
            dma((member_n, 2)),
            dma((member_n, 2)),
            dma((nb + 1, member_n)),
            dma((nb + 1, member_n)),
            dma((nb + 1,)),
            dma((ob,)),
            dma((ob,)),
            dma((ob, 4)),
            dma((ob, 4)),
            dma((nb + 1, member_n)),
            dma((nb + 1, member_n)),
            dma((nb + 1,)),
        ],
        compiler_params=pltpu.CompilerParams(
            vmem_limit_bytes=58 * 1024 * 1024, collective_id=0, has_side_effects=True
        ),
    )(obs_cell, op_select, obs_values, obs_weights, op_table, codes, states, loc_tiles)
    return copied(result)


def solution(mesh):
    placed = (
        P("member", "space"),
        P(),
        P(),
        P(None, "space", None),
        P(None, "space", None),
        P(),
        P(None, "space", "member", None),
        P(None, "space", "member", None),
        P(),
    )
    return jax.shard_map(
        per_device, mesh=mesh, in_specs=placed, out_specs=P("member", "space"), check_vma=False
    )
```
